32 devices in a mesh: dom: 8 (over z, x), bud: 4 (over y, core).
Axes of the slice: x: 2, y: 2, z: 4, core: 2. Of those that a mesh axis runs over, the one named last changes fastest.
Arguments:
- right_side: float32 [3, 32, 64, 128], P(None, 'dom', 'bud'), may hold values from -8 to 8
- stiffness: float32 [32, 64, 128], P('dom', 'bud'), may hold values from 0.5 to 2
- coupling: float32 [27, 3, 3], replicated, may hold values from -2 to 3, as said below
- iterate_in: float32 [3, 32, 64, 128], P(None, 'dom', 'bud'), may hold values from -8 to 8
- residual_in: float32 [3, 32, 64, 128], P(None, 'dom', 'bud'), may hold values from -20 to 20
- direction_in: float32 [3, 32, 64, 128], P(None, 'dom', 'bud'), may hold values from -20 to 20
- backup_in: float32 [2, 3, 32, 64, 128], P(None, None, 'dom', 'bud'), may hold values from -8 to 8
- beta_prev: float32 [1], replicated, may hold values from 0.3 to 0.9
- fail_column: int32 [8], P('dom'), may hold values from 0 to 3, as said below
- buddy_bit: int32 [8], P('dom'), may hold values from 0 to 1
Outputs:
- iterate: float32 [3, 32, 64, 128], P(None, 'dom', 'bud')
- residual: float32 [3, 32, 64, 128], P(None, 'dom', 'bud')
- backup: float32 [2, 3, 32, 64, 128], P(None, None, 'dom', 'bud')
The draws below stay inside these ranges and needn't reach their ends.
Inputs may be any that keep to these rules, and one draw needn't show every extreme that they name: `fail_column`: every column index appears among the lost columns. The buddy of block (i, k) is the block (i, k with binary digit buddy_bit[i] flipped). coupling[26 - o] is the transpose of coupling[o]; each diagonal entry of coupling[13] exceeds 1.02 times the sum of the magnitudes of all other entries of its row over all 27 blocks.
All inputs are finite; a program needn't handle non-finite values.
Results may differ from the reference program's by a relative error of at most 0.00015.
Values sent between devices are 32-bit elements; how exact they have to be, the bound alone decides.
A program may use at most 64 MiB of HBM per device.

```python
import math
import jax
import jax.numpy as jnp
import numpy as np
from jax import lax

CX = 4
CY = 16
SWEEPS = 4
NX = 32
NY = 64
NZ = 128
BLOCK_ROWS = 8
LEVELS = 2
N_DOM = 8
N_BUD = 4


def draw_fail_column(key, part):
    order = jax.random.permutation(jax.random.fold_in(key, 3), jnp.arange(BLOCK_ROWS, dtype=jnp.int32))
    return (order % N_BUD).astype(jnp.int32)


def draw_residual_in(key, part):
    random_part = jax.random.normal(jax.random.fold_in(key, 5), (3, NX, NY, NZ), jnp.float32)
    position = jnp.arange(NX, dtype=jnp.float32) / NX
    rising = 1.0 + 2.0 * position
    return jnp.clip(random_part * rising[None, :, None, None], -20.0, 20.0)


def draw_direction_in(key, part):
    random_part = jax.random.normal(jax.random.fold_in(key, 25), (3, NX, NY, NZ), jnp.float32)
    position = jnp.arange(NX, dtype=jnp.float32) / NX
    rising = 1.0 + 2.0 * position
    return jnp.clip(random_part * rising[None, :, None, None], -20.0, 20.0)


def draw_coupling(key, part):
    first_key, second_key, third_key = jax.random.split(jax.random.fold_in(key, 17), 3)
    identity = jnp.eye(3, dtype=jnp.float32)
    spread = jax.random.normal(first_key, (27, 3, 3), jnp.float32) * 0.25
    strength = jax.random.uniform(second_key, (27, 3), jnp.float32, 0.5, 1.5)
    drawn = spread * (1.0 - identity)[None] - strength[:, :, None] * identity[None]
    mirrored = 0.5 * (drawn + jnp.transpose(drawn[::-1], (0, 2, 1)))
    middle = jax.random.normal(third_key, (3, 3), jnp.float32) * 0.3
    middle = 0.5 * (middle + middle.T) * (1.0 - identity)
    outer_abs = jnp.sum(jnp.abs(mirrored), axis=(0, 2)) - jnp.sum(jnp.abs(mirrored[13]), axis=1)
    row_total = outer_abs + jnp.sum(jnp.abs(middle), axis=1)
    center_block = middle + identity * (1.02 * row_total)[:, None]
    coupled = mirrored.at[13].set(center_block)
    return coupled / jnp.mean(1.02 * row_total)


def with_ends(array, rng, least, top_value):
    longest = array.shape.index(max(array.shape))
    spots = []
    for shift in (0, 1):
        where = [jax.random.randint(jax.random.fold_in(rng, axis), (), 0, length) for axis, length in enumerate(array.shape)]
        where[longest] = (where[longest] + shift) % array.shape[longest]
        spots.append(tuple(where))
    return array.at[spots[0]].set(least).at[spots[1]].set(top_value)


def levels(rng, shape, cuts, low, top_value):
    def one(dim, blocks):
        heights = jax.random.uniform(jax.random.fold_in(jax.random.fold_in(rng, 6), dim), (blocks,), jnp.float32, low / len(cuts), top_value / len(cuts))
        return jnp.repeat(jnp.exp(heights), shape[dim] // blocks).reshape((-1,) + (1,) * (len(shape) - dim - 1))

    factor_of = one(*cuts[0])
    for cut in cuts[1:]:
        factor_of = factor_of * one(*cut)
    return factor_of


def centred(own_key, shape, scale, most, cuts=(), kind=jnp.bfloat16):
    array = scale * jax.random.normal(own_key, shape, jnp.float32)
    if cuts:
        array = array * levels(own_key, shape, cuts, -0.22, 0.18)
    return jnp.clip(array, -most, most).astype(kind)


def setup_inputs(seed: int = 0) -> dict:
    splits = jax.random.split(jax.random.key(seed), 11)
    right_side = centred(splits[0], (3, NX, NY, NZ), 1.0, 8.0, ((1, 8), (2, 4)), jnp.float32)
    stiffness = jnp.clip(jnp.exp(math.log(2.0) - 1.3862944 * jax.random.uniform(splits[1], (NX, NY, NZ), jnp.float32) ** levels(splits[1], (NX, NY, NZ), ((0, 8), (1, 4)), -0.2, 0.2)), 0.5, 2.0)
    coupling = draw_coupling(jax.random.fold_in(splits[10], 71), 0)
    iterate_in = centred(splits[3], (3, NX, NY, NZ), 1.0, 8.0, ((1, 8), (2, 4)), jnp.float32)
    residual_in = draw_residual_in(jax.random.fold_in(splits[10], 71), 0)
    direction_in = draw_direction_in(jax.random.fold_in(splits[10], 71), 0)
    backup_in = centred(splits[6], (2, 3, NX, NY, NZ), 1.0, 8.0, ((2, 8), (3, 4)), jnp.float32)
    beta_prev = jnp.clip(jax.random.uniform(splits[7], (1,), jnp.float32, 0.3, 0.9), 0.3, 0.9)
    fail_column = draw_fail_column(jax.random.fold_in(splits[10], 71), 0)
    buddy_bit = with_ends(jax.random.randint(splits[9], (BLOCK_ROWS,), 0, LEVELS), jax.random.fold_in(splits[9], 1), 0, LEVELS - 1).astype(jnp.int32)
    return dict(right_side=right_side, stiffness=stiffness, coupling=coupling, iterate_in=iterate_in, residual_in=residual_in, direction_in=direction_in, backup_in=backup_in, beta_prev=beta_prev, fail_column=fail_column, buddy_bit=buddy_bit)


LOW = 0.01
HIGH = 1.99


def stencil(padded, coupling):
    size_x = padded.shape[1] - 2
    size_y = padded.shape[2] - 2
    size_z = padded.shape[3] - 2
    summed = jnp.zeros((3, size_x, size_y, size_z), padded.dtype)
    for offset in range(27):
        shift_x = offset // 9
        shift_y = (offset // 3) % 3
        shift_z = offset % 3
        window = padded[:, shift_x:shift_x + size_x, shift_y:shift_y + size_y, shift_z:shift_z + size_z]
        summed = summed + jnp.einsum("ab,bxyz->axyz", coupling[offset], window, precision=lax.Precision.HIGHEST)
    return summed


def operate(vector, stiffness, coupling):
    scaled = vector * stiffness[None]
    padded = jnp.pad(scaled, ((0, 0), (1, 1), (1, 1), (1, 1)))
    return stencil(padded, coupling) * stiffness[None]


def pick_blocks(field, columns):
    shaped = field.reshape(3, N_DOM, CX, N_BUD, CY, NZ)
    picked = jnp.take_along_axis(shaped, columns[None, :, None, None, None, None], axis=3)[:, :, :, 0]
    return jnp.moveaxis(picked, 1, 0)


def place_blocks(blocks, base, lost_cells):
    spread = jnp.moveaxis(blocks, 0, 1)[:, :, :, None]
    spread = jnp.broadcast_to(spread, (3, N_DOM, CX, N_BUD, CY, NZ)).reshape(3, NX, NY, NZ)
    return jnp.where(lost_cells[None, :, :, None], spread, base)


def reference(right_side, stiffness, coupling, iterate_in, residual_in, direction_in, backup_in, beta_prev, fail_column, buddy_bit):
    center = jnp.diagonal(coupling[13])
    diagonal = stiffness[None] ** 2 * center[:, None, None, None]
    inverse = 1.0 / diagonal

    columns = fail_column.astype(jnp.int32)
    stride = jnp.left_shift(jnp.ones_like(columns), buddy_bit.astype(jnp.int32))
    buddy_columns = (columns + stride * (1 - 2 * ((columns // stride) % 2))).astype(jnp.int32)
    lost_rows = columns[:, None] == jnp.arange(N_BUD, dtype=jnp.int32)[None, :]
    lost_cells = jnp.broadcast_to(lost_rows[:, None, :, None], (N_DOM, CX, N_BUD, CY)).reshape(NX, NY)

    saved_prev = pick_blocks(backup_in[0], buddy_columns)
    saved_dir = pick_blocks(backup_in[1], buddy_columns)
    right_blocks = pick_blocks(right_side, columns)
    stiff_shaped = stiffness.reshape(N_DOM, CX, N_BUD, CY, NZ)
    stiff_blocks = jnp.take_along_axis(stiff_shaped, columns[:, None, None, None, None], axis=2)[:, :, 0]

    zeroed = jnp.where(lost_cells[None, :, :, None], 0.0, iterate_in)
    outside_all = operate(zeroed, stiffness, coupling)
    outer_blocks = pick_blocks(outside_all, columns)

    def rebuild_one(right_block, stiff_block, prev_block, dir_block, outer_term):
        diag_block = stiff_block[None] ** 2 * center[:, None, None, None]
        inverse_block = 1.0 / diag_block
        restored_z = dir_block - beta_prev[0] * prev_block
        restored_r = diag_block * restored_z
        target = right_block - restored_r - outer_term
        centre_value = (HIGH + LOW) / 2.0
        half_width = (HIGH - LOW) / 2.0
        ratio_value = centre_value / half_width
        recursion_weight = 1.0 / ratio_value
        update = inverse_block * target / centre_value
        solved = jnp.zeros_like(target)
        for sweep in range(SWEEPS):
            solved = solved + update
            if sweep < SWEEPS - 1:
                remain = target - operate(solved, stiff_block, coupling)
                weight_next = 1.0 / (2.0 * ratio_value - recursion_weight)
                update = weight_next * recursion_weight * update + (2.0 * weight_next / half_width) * inverse_block * remain
                recursion_weight = weight_next
        return solved, restored_r

    solved_blocks, restored_blocks = jax.vmap(rebuild_one)(right_blocks, stiff_blocks, saved_prev, saved_dir, outer_blocks)

    start_iter = place_blocks(solved_blocks, iterate_in, lost_cells)
    residual = place_blocks(restored_blocks, residual_in, lost_cells)
    direction = place_blocks(saved_dir, direction_in, lost_cells)

    preconditioned = inverse * residual
    norm_first = jnp.sum(residual * preconditioned)
    product_image = operate(direction, stiffness, coupling)
    alpha_first = norm_first / jnp.sum(direction * product_image)
    iterate_mid = start_iter + alpha_first * direction
    residual = residual - alpha_first * product_image
    preconditioned = inverse * residual
    norm_second = jnp.sum(residual * preconditioned)
    beta_first = norm_second / norm_first
    second_dir = preconditioned + beta_first * direction
    product_image = operate(second_dir, stiffness, coupling)
    alpha_second = norm_second / jnp.sum(second_dir * product_image)
    final_iterate = iterate_mid + alpha_second * second_dir
    final_residual = residual - alpha_second * product_image

    stacked = jnp.stack([direction, second_dir])
    blocks = stacked.reshape(2, 3, N_DOM, CX, N_BUD, CY, NZ)
    column_ids = np.arange(N_BUD)
    backup_blocks = jnp.zeros_like(blocks)
    for bit_level in range(LEVELS):
        level_stride = 2 ** bit_level
        partner = column_ids + level_stride * (1 - 2 * ((column_ids // level_stride) % 2))
        candidate = blocks[:, :, :, :, partner]
        chosen = (buddy_bit == bit_level)[None, None, :, None, None, None, None]
        backup_blocks = jnp.where(chosen, candidate, backup_blocks)
    backup = backup_blocks.reshape(2, 3, NX, NY, NZ)
    return (final_iterate, final_residual, backup)
```

```python
import functools

import jax
import jax.numpy as jnp
from jax import lax
from jax.experimental import pallas as pl
from jax.experimental.pallas import tpu as pltpu
from jax.sharding import PartitionSpec as P

SWEEPS = 4
LOW = 0.01
HIGH = 1.99
SIDES = [(sx, sy) for sx in (-1, 0, 1) for sy in (-1, 0, 1) if (sx, sy) != (0, 0)]
Y0 = 8


def kernel(
    nd, nb, levels,
    rhs_h, stiff_h, cpl_h, x_h, r_h, p_h, bk, beta_h, fc_h, bb_h,
    x_out, r0, bsend, b_out, img, s_out, coef,
    rhs, stiff, cpl, x_in, r_in, p_in, beta, fc, bb, in_sems,
    pads, padl, flat, ysend, yrecv, csend, crecv, saved, brecv,
    inv, img3, target, solved, update,
    red, red1, rall,
    hs, hr, ss, sr, bs, br, ds, dr, know,
):
    nx, ny, nz = stiff.shape
    step = 2 if nx % 2 == 0 else 1
    dom, bud = lax.axis_index("dom"), lax.axis_index("bud")

    def has(side):
        sx, sy = side
        ok = None
        for cond in (
            ([dom > 0] if sx < 0 else [dom < nd - 1] if sx > 0 else [])
            + ([bud > 0] if sy < 0 else [bud < nb - 1] if sy > 0 else [])
        ):
            ok = cond if ok is None else jnp.logical_and(ok, cond)
        return ok

    def remote(src, dst, send, recv, d, b):
        return pltpu.make_async_remote_copy(
            src_ref=src, dst_ref=dst, send_sem=send, recv_sem=recv,
            device_id={"dom": d, "bud": b}, device_id_type=pl.DeviceIdType.MESH,
        )

    def flip(level):
        stride = 1 << level
        return bud + stride * (1 - 2 * (lax.rem(bud // stride, 2)))

    barrier = pltpu.get_barrier_semaphore()

    def greet(sem, d, b):
        pl.semaphore_signal(
            sem, inc=1, device_id={"dom": d, "bud": b},
            device_id_type=pl.DeviceIdType.MESH,
        )

    def ahead(stride):
        return jnp.where(dom >= stride, 1, 0) + jnp.where(dom < nd - stride, 1, 0)

    def greet_dom(sem, stride):
        @pl.when(dom >= stride)
        def _():
            greet(sem, dom - stride, bud)

        @pl.when(dom < nd - stride)
        def _():
            greet(sem, dom + stride, bud)

    def greet_near(sem):
        greet_dom(sem, 1)
        for j in range(1, nb):
            greet(sem, dom, lax.rem(bud + j, nb))

    strides = [1 << i for i in range(max(nd - 1, 1).bit_length())]
    coef[...] = jnp.zeros(coef.shape, coef.dtype)
    loads = {}
    for i, (name, src, dst) in enumerate((
        ("cpl", cpl_h, cpl), ("fc", fc_h, fc), ("bb", bb_h, bb), ("beta", beta_h, beta),
        ("stiff", stiff_h, stiff), ("x", x_h, x_in),
        ("p", p_h, p_in), ("r", r_h, r_in), ("rhs", rhs_h, rhs),
    )):
        loads[name] = pltpu.make_async_copy(src, dst, in_sems.at[i])
        loads[name].start()

    for pad in [pads.at[e] for e in range(4)] + [padl]:
        face = jnp.zeros((3, ny + 2 * Y0, nz), pad.dtype)
        pad[:, 0] = face
        pad[:, nx + 1] = face
        rim = jnp.zeros((3, nx, Y0, nz), pad.dtype)
        pad[:, 1:nx + 1, 0:Y0, :] = rim
        pad[:, 1:nx + 1, Y0 + ny:ny + 2 * Y0, :] = rim
    yrecv[...] = jnp.zeros(yrecv.shape, yrecv.dtype)
    crecv[...] = jnp.zeros(crecv.shape, crecv.dtype)
    greet_near(barrier)

    for name in ("cpl", "fc", "bb", "stiff", "x"):
        loads[name].wait()
    me_failed = jnp.full((1, ny, nz), fc[0], jnp.int32) == bud
    bit_here = jnp.full((1, ny, nz), bb[0], jnp.int32)

    def halo_copies(e, which, side):
        sx, sy = side
        i = SIDES.index(side)
        o = SIDES.index((-sx, -sy))
        to = (dom + sx, bud + sy)
        if sy == 0:
            src = flat.at[e, :, nx - 1 if sx > 0 else 0]
            dst = pads.at[e, :, 0 if sx > 0 else nx + 1, pl.ds(Y0, ny), :]
        elif sx == 0:
            src = ysend.at[e, 1 if sy > 0 else 0]
            dst = yrecv.at[e, 0 if sy > 0 else 1]
        else:
            src = csend.at[e, i]
            dst = crecv.at[e, o]
        return remote(src, dst, hs.at[e, i], hr.at[e, o], *to)

    def landing(e, side):
        sx, sy = side
        i = SIDES.index(side)
        if sy == 0:
            src = flat.at[e, :, nx - 1 if sx > 0 else 0]
            dst = pads.at[e, :, nx + 1 if sx > 0 else 0, pl.ds(Y0, ny), :]
        elif sx == 0:
            src = ysend.at[e, 1 if sy > 0 else 0]
            dst = yrecv.at[e, 1 if sy > 0 else 0]
        else:
            src = csend.at[e, i]
            dst = crecv.at[e, i]
        return remote(src, dst, hs.at[e, i], hr.at[e, i], dom + sx, bud + sy)

    def pack(e, corners=None):
        for c in range(3):
            for x in range(nx if corners is not True else 0):
                row = c * nx + x
                ysend[e, 0, row:row + 1, :] = flat[e, c, x, 0:1, :]
                ysend[e, 1, row:row + 1, :] = flat[e, c, x, ny - 1:ny, :]
            for i, (sx, sy) in enumerate(SIDES):
                if sx != 0 and sy != 0 and corners is not False:
                    y = ny - 1 if sy > 0 else 0
                    csend[e, i, c:c + 1, :] = flat[e, c, nx - 1 if sx > 0 else 0, y:y + 1, :]

    def send_halo(e, sides=SIDES):
        for side in sides:
            @pl.when(has(side))
            def _(side=side):
                halo_copies(e, 0, side).start()

    def take_halo(e):
        for side in SIDES:
            @pl.when(has(side))
            def _(side=side):
                landing(e, side).wait_recv()
        for c in range(3):
            for x in range(nx):
                row = c * nx + x
                pads[e, c, x + 1, Y0 - 1:Y0, :] = yrecv[e, 0, row:row + 1, :]
                pads[e, c, x + 1, Y0 + ny:Y0 + ny + 1, :] = yrecv[e, 1, row:row + 1, :]
            for i, (sx, sy) in enumerate(SIDES):
                if sx != 0 and sy != 0:
                    y = Y0 + ny if sy > 0 else Y0 - 1
                    pads[e, c, nx + 1 if sx > 0 else 0, y:y + 1, :] = crecv[e, i, c:c + 1, :]

    def end_halo(e):
        for side in SIDES:
            @pl.when(has(side))
            def _(side=side):
                halo_copies(e, 0, side).wait_send()

    lane = lax.broadcasted_iota(jnp.int32, (step, ny, nz), 2)

    def apply(pad, out):
        @pl.loop(0, nx // step)
        def _(j):
            x = j * step
            acc = [[None] * 3 for _ in range(3)]
            for dx in range(3):
                for dy in range(3):
                    for b in range(3):
                        w = pad[b, pl.ds(x + dx, step), Y0 - 1 + dy:Y0 - 1 + dy + ny, :]
                        for dz in range(3):
                            o = (dx * 3 + dy) * 3 + dz
                            for a in range(3):
                                term = cpl[a, b, o] * w
                                acc[dz][a] = term if acc[dz][a] is None else acc[dz][a] + term
            for a in range(3):
                before = jnp.where(lane == 0, 0.0, pltpu.roll(acc[0][a], 1, 2))
                after = jnp.where(lane == nz - 1, 0.0, pltpu.roll(acc[2][a], nz - 1, 2))
                out[a, pl.ds(x, step)] = acc[1][a] + before + after

    centre = [cpl[a, a, 13] for a in range(3)]

    for a in range(3):
        scaled = jnp.where(me_failed, 0.0, x_in[a] * stiff[...])
        flat[0, a] = scaled
        pads[0, a, 1:nx + 1, Y0:Y0 + ny, :] = scaled
        inv[a] = 1.0 / (stiff[...] * stiff[...] * centre[a])
    pack(0)

    pl.semaphore_wait(barrier, nb - 1 + ahead(1))
    greet_near(know.at[0])

    pieces = [(0, pl.ds(0, nx)), (1, pl.ds(0, 1)), (1, pl.ds(nx - 1, 1)), (1, pl.ds(1, nx - 2))]
    fetch = [[remote(bk.at[w, :, x], saved.at[l, w, :, x], ss.at[l, i], sr.at[l, i], dom, flip(l))
              for l in range(levels)] for i, (w, x) in enumerate(pieces)]
    for i in (1, 2, 3):
        for l in range(levels):
            fetch[i][l].start()
    send_halo(0, [s for s in SIDES if s[0] == 0 or s[1] == 0])
    for l in range(levels):
        fetch[0][l].start()
    pl.semaphore_wait(know.at[0], nb - 1 + ahead(1))
    for i, stride in enumerate(strides[1:2]):
        greet_dom(know.at[1], stride)
    send_halo(0, [s for s in SIDES if s[0] != 0 and s[1] != 0])

    keep = [[remote(bsend.at[w], brecv.at[l, w], bs.at[l, w], br.at[l, w], dom, flip(l))
             for l in range(levels)] for w in range(3)]

    def pick(buf, w, a):
        value = buf[0, w, a]
        for l in range(1, levels):
            value = jnp.where(bit_here == l, buf[l, w, a], value)
        return value

    def start_field(x):
        for a in range(3):
            got = saved[0, 1, a, x]
            for l in range(1, levels):
                got = jnp.where(bit_here == l, saved[l, 1, a, x], got)
            p0 = jnp.where(me_failed, got, p_in[a, x])
            bsend[0, a, x] = p0
            u0 = p0 * stiff[x]
            flat[1, a, x] = u0
            pads[1, a, x.start + 1:x.stop + 1, Y0:Y0 + ny, :] = u0

    loads["p"].wait()
    for i in (1, 2):
        for l in range(levels):
            fetch[i][l].wait_recv()
    start_field(slice(0, 1))
    start_field(slice(nx - 1, nx))
    pack(1, True)
    send_halo(1, [s for s in SIDES if s[0] != 0])
    for l in range(levels):
        fetch[3][l].wait_recv()
    start_field(slice(1, nx - 1))
    pack(1, False)
    send_halo(1, [s for s in SIDES if s[0] == 0])
    for l in range(levels):
        keep[0][l].start()
    for i in range(1, len(strides)):
        pl.semaphore_wait(know.at[i], ahead(strides[i]))
        if i + 1 < len(strides):
            greet_dom(know.at[i + 1], strides[i + 1])
    for name in ("r", "rhs", "beta"):
        loads[name].wait()
    for l in range(levels):
        fetch[0][l].wait_recv()
    for a in range(3):
        restored_z = pick(saved, 1, a) - beta[0] * pick(saved, 0, a)
        restored_r = restored_z * (stiff[...] * stiff[...] * centre[a])
        z0 = jnp.where(me_failed, restored_z, inv[a] * r_in[a])
        r0[a] = jnp.where(me_failed, restored_r, r_in[a])
        target[a] = rhs[a] - restored_r
        bsend[1, a] = z0
        a0 = z0 * stiff[...]
        flat[2, a] = a0
        pads[2, a, 1:nx + 1, Y0:Y0 + ny, :] = a0
    pack(2)
    send_halo(2)

    take_halo(1)
    apply(pads.at[1], img.at[0])
    for a in range(3):
        b0 = img[0, a] * (1.0 / jnp.full((1, ny, nz), centre[a], jnp.float32))
        flat[3, a] = b0
        pads[3, a, 1:nx + 1, Y0:Y0 + ny, :] = b0
    pack(3)
    send_halo(3)
    for a in range(3):
        bsend[2, a] = flat[3, a] / stiff[...]
    for w in (1, 2):
        for l in range(levels):
            keep[w][l].start()

    take_halo(2)
    apply(pads.at[2], img.at[1])
    take_halo(0)
    apply(pads.at[0], img3)
    def dot(*terms):
        total = None
        for a in range(3):
            for v in terms:
                t = v(a)
                total = t if total is None else total + t
        return jnp.sum(jnp.sum(total, axis=0), axis=0, keepdims=True)

    red[...] = jnp.zeros(red.shape, red.dtype)
    red[0:1, :] = dot(lambda a: r0[a] * bsend[1, a])
    red[1:2, :] = dot(lambda a: flat[1, a] * img[0, a])
    red[2:3, :] = dot(lambda a: flat[2, a] * img[0, a])
    red[3:4, :] = dot(lambda a: flat[3, a] * img[0, a])
    red[4:5, :] = dot(lambda a: flat[2, a] * img[1, a])
    red[5:6, :] = dot(lambda a: flat[3, a] * img[1, a])
    take_halo(3)
    apply(pads.at[3], img.at[2])
    red[6:7, :] = dot(lambda a: flat[3, a] * img[2, a])

    rows = lax.broadcasted_iota(jnp.int32, (8, nz), 0)
    diagonal = rows == lax.broadcasted_iota(jnp.int32, (8, nz), 1)
    each = jnp.sum(red[...], axis=1, keepdims=True)
    red1[...] = jnp.sum(jnp.where(diagonal, each, 0.0), axis=0, keepdims=True)
    n = nd * nb
    me = dom * nb + bud
    rall[me] = red1[...]
    order = sorted(range(1, n), key=lambda j: abs(2 * j - n))
    for j in order:
        peer = lax.rem(me + j, n)
        remote(red1, rall.at[me], ds.at[0], dr.at[0], peer // nb, lax.rem(peer, nb)).start()

    def every():
        part = rall.at[pl.ds(0, n - 1)]
        return remote(part, part, ds.at[0], dr.at[0], dom, bud)

    centre_value = (HIGH + LOW) / 2.0
    half_width = (HIGH - LOW) / 2.0
    ratio_value = centre_value / half_width
    weight = 1.0 / ratio_value
    for a in range(3):
        t = target[a] - img3[a] * stiff[...]
        d = inv[a] * t / centre_value
        target[a] = t
        update[a] = d
        solved[a] = d
        padl[a, 1:nx + 1, Y0:Y0 + ny, :] = d * stiff[...]
    for sweep in range(SWEEPS - 1):
        apply(padl, img3)
        weight_next = 1.0 / (2.0 * ratio_value - weight)
        for a in range(3):
            remain = target[a] - img3[a] * stiff[...]
            d = weight_next * weight * update[a] + (2.0 * weight_next / half_width) * (inv[a] * remain)
            y = solved[a] + d
            update[a] = d
            solved[a] = y
            if sweep < SWEEPS - 2:
                padl[a, 1:nx + 1, Y0:Y0 + ny, :] = y * stiff[...]
        weight = weight_next

    for w in range(3):
        for l in range(levels):
            keep[w][l].wait_recv()
    for a in range(3):
        x_out[a] = jnp.where(me_failed, solved[a], x_in[a])
        for w in range(3):
            b_out[w, a] = pick(brecv, w, a)
    s_out[...] = stiff[...]
    for e in range(4):
        end_halo(e)
    every().wait_recv()
    total = jnp.sum(rall[...], axis=0)
    sums = jnp.sum(jnp.where(diagonal, jnp.broadcast_to(total, (8, nz)), 0.0), axis=1, keepdims=True)
    g0, c0, e0, f0, h0, h1, h2 = [jnp.broadcast_to(sums[j:j + 1], (1, nz)) for j in range(7)]
    alpha0 = g0 / c0
    g1 = g0 - 2.0 * alpha0 * e0 + alpha0 * alpha0 * f0
    beta0 = g1 / g0
    c1 = (
        h0 - 2.0 * alpha0 * h1 + alpha0 * alpha0 * h2
        + 2.0 * beta0 * (e0 - alpha0 * f0) + beta0 * beta0 * c0
    )
    alpha1 = g1 / c1
    coef[0:1, :] = alpha0
    coef[1:2, :] = beta0
    coef[2:3, :] = alpha1

    for i in range(4):
        for l in range(levels):
            fetch[i][l].wait_send()
    for w in range(3):
        for l in range(levels):
            keep[w][l].wait_send()
    every().wait_send()


def finish(x0, r0, own, other, img, stiff, coef, x_out, r_out, b_out, xs, rs, bs, sems):
    copies = [pltpu.make_async_copy(other.at[0], b_out.at[0], sems.at[9])]
    copies[0].start()
    alpha0, beta0, alpha1 = coef[0:1, :], coef[1:2, :], coef[2:3, :]
    alpha0, beta0, alpha1 = alpha0[None], beta0[None], alpha1[None]
    for a in range(3):
        bs[a] = other[1, a] - alpha0 * other[2, a] + beta0 * other[0, a]
        p0 = own[0, a]
        p1 = own[1, a] - alpha0 * own[2, a] + beta0 * p0
        xs[a] = x0[a] + alpha0 * p0 + alpha1 * p1
        t0 = img[0, a]
        q1 = img[1, a] - alpha0 * img[2, a] + beta0 * t0
        rs[a] = r0[a] - stiff[...] * (alpha0 * t0 + alpha1 * q1)
        for i, (src, dst) in enumerate((
            (bs.at[a], b_out.at[1, a]), (xs.at[a], x_out.at[a]), (rs.at[a], r_out.at[a]),
        )):
            copies.append(pltpu.make_async_copy(src, dst, sems.at[a * 3 + i]))
            copies[-1].start()
    for c in copies:
        c.wait()


def on_device(nd, nb, rhs, stiff, coupling, x_in, r_in, p_in, backup_in, beta, fc, bb):
    levels = nb.bit_length() - 1
    nx, ny, nz = stiff.shape
    f32 = jnp.float32
    rows = -(-3 * nx // 8) * 8
    vmem = pl.BlockSpec(memory_space=pltpu.VMEM)
    hbm = pl.BlockSpec(memory_space=pltpu.HBM)
    field = (3, nx, ny, nz)
    dma = pltpu.SemaphoreType.DMA
    parts = pl.pallas_call(
        functools.partial(kernel, nd, nb, levels),
        out_shape=(
            pltpu.VMEM(field, f32),
            pltpu.VMEM(field, f32),
            pltpu.VMEM((3,) + field, f32),
            pltpu.VMEM((3,) + field, f32),
            pltpu.VMEM((3,) + field, f32),
            pltpu.VMEM((nx, ny, nz), f32),
            pltpu.VMEM((8, nz), f32),
        ),
        in_specs=[hbm] * 7 + [pl.BlockSpec(memory_space=pl.ANY)] * 3,
        out_specs=(vmem,) * 7,
        scratch_shapes=[
            pltpu.VMEM(field, f32),
            pltpu.VMEM((nx, ny, nz), f32),
            pltpu.SMEM((3, 3, 27), f32),
            pltpu.VMEM(field, f32),
            pltpu.VMEM(field, f32),
            pltpu.VMEM(field, f32),
            pltpu.SMEM((1,), f32),
            pltpu.SMEM((1,), jnp.int32),
            pltpu.SMEM((1,), jnp.int32),
            dma((9,)),
            pltpu.VMEM((4, 3, nx + 2, ny + 2 * Y0, nz), f32),
            pltpu.VMEM((3, nx + 2, ny + 2 * Y0, nz), f32),
            pltpu.VMEM((4,) + field, f32),
            pltpu.VMEM((4, 2, rows, nz), f32),
            pltpu.VMEM((4, 2, rows, nz), f32),
            pltpu.VMEM((4, 8, 8, nz), f32),
            pltpu.VMEM((4, 8, 8, nz), f32),
            pltpu.VMEM((levels, 2) + field, f32),
            pltpu.VMEM((levels, 3) + field, f32),
            pltpu.VMEM(field, f32),
            pltpu.VMEM(field, f32),
            pltpu.VMEM(field, f32),
            pltpu.VMEM(field, f32),
            pltpu.VMEM(field, f32),
            pltpu.VMEM((8, nz), f32),
            pltpu.VMEM((1, nz), f32),
            pltpu.VMEM((nd * nb, 1, nz), f32),
            dma((4, 8)), dma((4, 8)),
            dma((levels, 4)), dma((levels, 4)),
            dma((levels, 3)), dma((levels, 3)),
            dma((1,)), dma((1,)),
            pltpu.SemaphoreType.REGULAR((nd.bit_length(),)),
        ],
        compiler_params=pltpu.CompilerParams(
            collective_id=0, has_side_effects=True, vmem_limit_bytes=40 * 1024 * 1024
        ),
    )(*[pltpu.with_memory_space_constraint(v, pltpu.HBM) for v in (
        rhs, stiff, jnp.transpose(coupling, (1, 2, 0)), x_in, r_in, p_in, backup_in
    )], beta, fc, bb)
    return pl.pallas_call(
        finish,
        out_shape=(
            pltpu.HBM(field, f32), pltpu.HBM(field, f32), pltpu.HBM((2,) + field, f32),
        ),
        in_specs=[vmem] * 7,
        out_specs=(hbm, hbm, hbm),
        scratch_shapes=[
            pltpu.VMEM(field, f32), pltpu.VMEM(field, f32), pltpu.VMEM(field, f32), dma((10,)),
        ],
        compiler_params=pltpu.CompilerParams(vmem_limit_bytes=8 * 1024 * 1024),
    )(*parts)


def solution(mesh):
    nd, nb = mesh.shape["dom"], mesh.shape["bud"]
    placed = (
        P(None, "dom", "bud", None),
        P("dom", "bud", None),
        P(),
        P(None, "dom", "bud", None),
        P(None, "dom", "bud", None),
        P(None, "dom", "bud", None),
        P(None, None, "dom", "bud", None),
        P(),
        P("dom"),
        P("dom"),
    )
    return jax.shard_map(
        functools.partial(on_device, nd, nb),
        mesh=mesh,
        in_specs=placed,
        out_specs=(
            P(None, "dom", "bud", None),
            P(None, "dom", "bud", None),
            P(None, None, "dom", "bud", None),
        ),
        check_vma=False,
    )
```

```python
import functools

import jax
import jax.numpy as jnp
from jax import lax
from jax.experimental import pallas as pl
from jax.experimental.pallas import tpu as pltpu
from jax.sharding import PartitionSpec as P

SWEEPS = 4
LOW = 0.01
HIGH = 1.99
Y0 = 8
CORNERS = [(sx, sy) for sx in (-1, 1) for sy in (-1, 1)]


class Halo:
    def __init__(self, depth, pad, ysend, yrecv, csend, crecv, send, recv):
        self.depth, self.pad = depth, pad
        self.ysend, self.yrecv, self.csend, self.crecv = ysend, yrecv, csend, crecv
        self.send, self.recv = send, recv


def halo_sems(depth):
    return 6 * depth + 2


def kernel(
    nd, nb, levels,
    rhs_h, stiff_h, cpl_h, x_h, r_h, p_h, bk_h, beta, fc, bb,
    x_out, r0, own, other, img, s_out, coef,
    rhs, stiff, cpl, x_in, r_in, p_in, bk, in_sems,
    upad, apad, xpad, bpad, lpad,
    yus, yur, cus, cur, yas, yar, cas, car, yxs, yxr, cxs, cxr,
    edge, edge_out, saved, brecv,
    inv, invs, img3, target, solved, update,
    red, red1, rall,
    us, ur, as_, ar, xs, xr, ss, sr, bs, br, ds, dr, know,
):
    nx, ny, nz = stiff.shape
    step = 2 if nx % 2 == 0 else 1
    dom, bud = lax.axis_index("dom"), lax.axis_index("bud")
    f32 = jnp.float32

    def has(sx, sy):
        ok = None
        for cond in (
            ([dom > 0] if sx < 0 else [dom < nd - 1] if sx > 0 else [])
            + ([bud > 0] if sy < 0 else [bud < nb - 1] if sy > 0 else [])
        ):
            ok = cond if ok is None else jnp.logical_and(ok, cond)
        return ok

    def remote(src, dst, send, recv, d, b):
        return pltpu.make_async_remote_copy(
            src_ref=src, dst_ref=dst, send_sem=send, recv_sem=recv,
            device_id={"dom": d, "bud": b}, device_id_type=pl.DeviceIdType.MESH,
        )

    def flip(level):
        stride = 1 << level
        return bud + stride * (1 - 2 * (lax.rem(bud // stride, 2)))

    barrier = pltpu.get_barrier_semaphore()

    def greet(sem, d, b):
        pl.semaphore_signal(
            sem, inc=1, device_id={"dom": d, "bud": b},
            device_id_type=pl.DeviceIdType.MESH,
        )

    def ahead(stride):
        return jnp.where(dom >= stride, 1, 0) + jnp.where(dom < nd - stride, 1, 0)

    def greet_dom(sem, stride):
        @pl.when(dom >= stride)
        def _():
            greet(sem, dom - stride, bud)

        @pl.when(dom < nd - stride)
        def _():
            greet(sem, dom + stride, bud)

    def greet_near(sem):
        greet_dom(sem, 1)
        for j in range(1, nb):
            greet(sem, dom, lax.rem(bud + j, nb))

    strides = [1 << i for i in range(max(nd - 1, 1).bit_length())]
    greet_near(barrier)

    loads = {}
    for i, (name, src, dst) in enumerate((
        ("cpl", cpl_h, cpl), ("bk", bk_h, bk), ("stiff", stiff_h, stiff), ("x", x_h, x_in),
        ("p", p_h, p_in), ("r", r_h, r_in), ("rhs", rhs_h, rhs),
    )):
        loads[name] = pltpu.make_async_copy(src, dst, in_sems.at[i])
        loads[name].start()

    U = Halo(2, upad, yus, yur, cus, cur, us, ur)
    A = Halo(1, apad, yas, yar, cas, car, as_, ar)
    X = Halo(1, xpad, yxs, yxr, cxs, cxr, xs, xr)
    inner = pl.ds(Y0, ny)

    for h in (U, A, X):
        deep = h.depth
        for sx in (-1, 1):
            @pl.when(jnp.logical_not(has(sx, 0)))
            def _(h=h, deep=deep, sx=sx):
                for d in range(deep):
                    x = deep - 1 - d if sx < 0 else deep + nx + d
                    h.pad[:, x, inner, :] = jnp.zeros((3, ny, nz), f32)

        for sy in (-1, 1):
            @pl.when(jnp.logical_not(has(0, sy)))
            def _(h=h, sy=sy):
                i = 1 if sy > 0 else 0
                h.yrecv[i] = jnp.zeros(h.yrecv.shape[1:], f32)

        for q, (sx, sy) in enumerate(CORNERS):
            @pl.when(jnp.logical_not(has(sx, sy)))
            def _(h=h, q=q):
                h.crecv[q] = jnp.zeros(h.crecv.shape[1:], f32)

    def xface(h, sx, d):
        deep = h.depth
        src = deep + (nx - 1 - d if sx > 0 else d)
        dst = deep - 1 - d if sx > 0 else deep + nx + d
        i, o = (deep + d, d) if sx > 0 else (d, deep + d)
        return remote(
            h.pad.at[:, src, inner, :], h.pad.at[:, dst, inner, :],
            h.send.at[i], h.recv.at[o], dom + sx, bud,
        )

    def yface(h, sy):
        i, o = (1, 0) if sy > 0 else (0, 1)
        return remote(
            h.ysend.at[i], h.yrecv.at[o],
            h.send.at[2 * h.depth + i], h.recv.at[2 * h.depth + o], dom, bud + sy,
        )

    def corner(h, q, e):
        sx, sy = CORNERS[q]
        base = 2 * h.depth + 2
        return remote(
            h.csend.at[q, e], h.crecv.at[3 - q, e],
            h.send.at[base + q * h.depth + e], h.recv.at[base + (3 - q) * h.depth + e],
            dom + sx, bud + sy,
        )

    def xland(h, sx, d):
        deep = h.depth
        x = deep + nx + d if sx > 0 else deep - 1 - d
        i = deep + d if sx > 0 else d
        part = h.pad.at[:, x, inner, :]
        return remote(part, part, h.send.at[i], h.recv.at[i], dom + sx, bud)

    def yland(h, sy):
        i = 1 if sy > 0 else 0
        part = h.yrecv.at[i]
        return remote(part, part, h.send.at[2 * h.depth + i], h.recv.at[2 * h.depth + i], dom, bud + sy)

    def cland(h, q, e):
        sx, sy = CORNERS[q]
        i = 2 * h.depth + 2 + q * h.depth + e
        part = h.crecv.at[q, e]
        return remote(part, part, h.send.at[i], h.recv.at[i], dom + sx, bud + sy)

    def each_x(h, d, do):
        for sx in (-1, 1):
            @pl.when(has(sx, 0))
            def _(sx=sx):
                do(h, sx, d)

    def each_y(h, do):
        for sy in (-1, 1):
            @pl.when(has(0, sy))
            def _(sy=sy):
                do(h, sy)

    def each_c(h, e, do):
        for q, (sx, sy) in enumerate(CORNERS):
            @pl.when(has(sx, sy))
            def _(q=q):
                do(h, q, e)

    def pack_y(h):
        deep = h.depth
        for i in range(2):
            for b in range(3):
                for d in range(deep):
                    y = Y0 + (ny - deep + d if i else d)
                    for x in range(nx):
                        h.ysend[i, b, d, x:x + 1, :] = h.pad[b, deep + x, y:y + 1, :]

    def pack_c(h, e):
        deep = h.depth
        for q, (sx, sy) in enumerate(CORNERS):
            x = deep + (nx - 1 - e if sx > 0 else e)
            for b in range(3):
                for d in range(deep):
                    y = Y0 + (ny - deep + d if sy > 0 else d)
                    h.csend[q, e, b, d:d + 1, :] = h.pad[b, x, y:y + 1, :]

    def unpack_y(h):
        deep = h.depth
        for i in range(2):
            y, d = (Y0 + ny, 0) if i else (Y0 - 1, deep - 1)
            for b in range(3):
                for x in range(nx):
                    h.pad[b, deep + x, y:y + 1, :] = h.yrecv[i, b, d, x:x + 1, :]

    def unpack_c(h, e):
        deep = h.depth
        for q, (sx, sy) in enumerate(CORNERS):
            x = deep + nx + e if sx > 0 else deep - 1 - e
            y, d = (Y0 + ny, 0) if sy > 0 else (Y0 - 1, deep - 1)
            for b in range(3):
                h.pad[b, x, y:y + 1, :] = h.crecv[q, e, b, d:d + 1, :]

    def start_x(h, d):
        each_x(h, d, lambda *a: xface(*a).start())

    def start_y(h):
        each_y(h, lambda *a: yface(*a).start())

    def start_c(h, e):
        each_c(h, e, lambda *a: corner(*a).start())

    def take(h, d):
        each_x(h, d, lambda *a: xland(*a).wait_recv())
        each_c(h, d, lambda *a: cland(*a).wait_recv())
        if d == 0:
            each_y(h, lambda *a: yland(*a).wait_recv())
            unpack_y(h)
        unpack_c(h, d)

    def end(h):
        for d in range(h.depth):
            each_x(h, d, lambda *a: xface(*a).wait_send())
            each_c(h, d, lambda *a: corner(*a).wait_send())
        each_y(h, lambda *a: yface(*a).wait_send())

    def stencil(load, groups):
        acc = [[[None] * groups for _ in range(3)] for _ in range(3)]
        for dx in range(3):
            for dy in range(3):
                for b in range(3):
                    ws = [load(b, dx, dy, g) for g in range(groups)]
                    for dz in range(3):
                        o = (dx * 3 + dy) * 3 + dz
                        for a in range(3):
                            for g in range(groups):
                                term = cpl[a, b, o] * ws[g]
                                old = acc[dz][a][g]
                                acc[dz][a][g] = term if old is None else old + term
        lane = lax.broadcasted_iota(jnp.int32, acc[0][0][0].shape, 1)

        def joined(a, g):
            before = jnp.where(lane == 0, 0.0, pltpu.roll(acc[0][a][g], 1, 1))
            after = jnp.where(lane == nz - 1, 0.0, pltpu.roll(acc[2][a][g], nz - 1, 1))
            return acc[1][a][g] + before + after

        return [[joined(a, g) for g in range(groups)] for a in range(3)]

    def apply(pad, deep, out):
        @pl.loop(0, nx // step)
        def _(j):
            x = j * step
            got = stencil(
                lambda b, dx, dy, g: pad[b, x + (g + deep - 1 + dx), Y0 - 1 + dy:Y0 - 1 + dy + ny, :], step
            )
            for a in range(3):
                for g in range(step):
                    out[a, x + g] = got[a][g]

    for name in ("cpl", "stiff", "x", "bk"):
        loads[name].wait()
    me_failed = jnp.full((1, ny, nz), fc[0], jnp.int32) == bud
    bit_here = jnp.full((1, ny, nz), bb[0], jnp.int32)
    centre = [cpl[a, a, 13] for a in range(3)]
    for a in range(3):
        xpad[a, 1:nx + 1, inner, :] = jnp.where(me_failed, 0.0, x_in[a] * stiff[...])
    pack_y(X)
    pack_c(X, 0)

    pl.semaphore_wait(barrier, nb - 1 + ahead(1))

    pieces = [pl.ds(0, 1), pl.ds(nx - 1, 1), pl.ds(1, nx - 2)]
    fetch = [[[remote(bk.at[w, :, x], saved.at[l, w, :, x], ss.at[l, w, i], sr.at[l, w, i], dom, flip(l))
               for l in range(levels)] for i, x in enumerate(pieces)] for w in range(2)]
    for w in (1, 0):
        for i in range(3):
            for l in range(levels):
                fetch[w][i][l].start()
    greet_near(know.at[0])
    start_x(X, 0)
    start_y(X)

    coef[...] = jnp.zeros(coef.shape, f32)
    red[...] = jnp.zeros(red.shape, f32)
    for x in (0, nx + 1):
        lpad[:, x] = jnp.zeros((3, ny + 2 * Y0, nz), f32)
    for y in (0, Y0 + ny):
        lpad[:, 1:nx + 1, y:y + Y0, :] = jnp.zeros((3, nx, Y0, nz), f32)
    invs[...] = 1.0 / stiff[...]
    inv_centre = [1.0 / jnp.full((1, nz), centre[a], f32) for a in range(3)]
    for a in range(3):
        inv[a] = 1.0 / (stiff[...] * stiff[...] * centre[a])

    pl.semaphore_wait(know.at[0], nb - 1 + ahead(1))
    if len(strides) > 1:
        greet_dom(know.at[1], strides[1])
    start_c(X, 0)

    def pick(value, l_of):
        got = l_of(0)
        for l in range(1, levels):
            got = jnp.where(bit_here == l, l_of(l), got)
        return jnp.where(me_failed, got, value)

    def start_field(x):
        for a in range(3):
            p0 = pick(p_in[a, x], lambda l: saved[l, 1, a, x])
            own[0, a, x] = p0
            upad[a, x.start + 2:x.stop + 2, inner, :] = p0 * stiff[x]

    loads["p"].wait()
    for i in (0, 1):
        for l in range(levels):
            fetch[1][i][l].wait_recv()
    start_field(slice(0, 1))
    start_field(slice(nx - 1, nx))
    pack_c(U, 0)
    start_c(U, 0)
    start_x(U, 0)
    for l in range(levels):
        fetch[1][2][l].wait_recv()
    start_field(slice(1, nx - 1))
    pack_c(U, 1)
    start_c(U, 1)
    start_x(U, 1)
    pack_y(U)
    start_y(U)

    keep = [[[remote(own.at[w, :, x], brecv.at[l, w, :, x], bs.at[l, w, i], br.at[l, w, i], dom, flip(l))
              for l in range(levels)] for i, x in enumerate((pl.ds(0, nx // 2), pl.ds(nx // 2, nx - nx // 2)))]
            for w in range(3)]

    def start_keep(w, i):
        for l in range(levels):
            keep[w][i][l].start()

    start_keep(0, 0)
    for i in range(1, len(strides)):
        pl.semaphore_wait(know.at[i], ahead(strides[i]))
        if i + 1 < len(strides):
            greet_dom(know.at[i + 1], strides[i + 1])

    def second_field(x):
        for a in range(3):
            s = stiff[x]
            restored_z = pick(0.0, lambda l: saved[l, 1, a, x]) - beta[0] * pick(0.0, lambda l: saved[l, 0, a, x])
            restored_r = restored_z * (s * s * centre[a])
            z0 = jnp.where(me_failed, restored_z, inv[a, x] * r_in[a, x])
            r0[a, x] = jnp.where(me_failed, restored_r, r_in[a, x])
            target[a, x] = rhs[a, x] - restored_r
            own[1, a, x] = z0
            apad[a, x.start + 1:x.stop + 1, inner, :] = z0 * s

    for name in ("r", "rhs"):
        loads[name].wait()
    for i in (0, 1):
        for l in range(levels):
            fetch[0][i][l].wait_recv()
    second_field(slice(0, 1))
    second_field(slice(nx - 1, nx))
    pack_c(A, 0)
    start_c(A, 0)
    start_x(A, 0)
    for l in range(levels):
        fetch[0][2][l].wait_recv()
    second_field(slice(1, nx - 1))
    pack_y(A)
    start_y(A)
    start_keep(0, 1)
    start_keep(1, 0)
    start_keep(1, 1)

    take(U, 0)
    apply(upad, 2, img.at[0])
    for a in range(3):
        b0 = img[0, a] * inv_centre[a]
        bpad[a, 1:nx + 1, inner, :] = b0
        own[2, a] = b0 * invs[...]
    take(U, 1)
    for b in range(3):
        for i in range(2):
            for d in range(2):
                lev = i + d
                edge[i, b, lev, 2:nx + 2, :] = yur[i, b, d]
                for q, (sx, sy) in enumerate(CORNERS):
                    if (sy > 0) == bool(i):
                        for e in range(2):
                            x = nx + 2 + e if sx > 0 else 1 - e
                            edge[i, b, lev, x:x + 1, :] = cur[q, e, b, d:d + 1, :]
            y = Y0 + (ny - 1 if i else 0)
            for x in range(nx + 4):
                edge[i, b, 0 if i else 2, x:x + 1, :] = upad[b, x, y:y + 1, :]

    rim = stencil(lambda b, dx, dy, g: upad[b, (nx + 1 if g else 0) + dx, Y0 - 1 + dy:Y0 - 1 + dy + ny, :], 2)
    for a in range(3):
        for g, sx in enumerate((-1, 1)):
            b0 = rim[a][g] * inv_centre[a]
            bpad[a, nx + 1 if g else 0, inner, :] = jnp.where(has(sx, 0), b0, 0.0)
    rim = stencil(lambda b, dx, dy, g: edge[g, b, dy, dx:dx + nx + 2, :], 2)
    row = lax.broadcasted_iota(jnp.int32, (nx + 2, nz), 0)
    first_in = jnp.where(dom > 0, 0, 1)
    last_in = jnp.where(dom < nd - 1, nx + 1, nx)
    inside = jnp.logical_and(row >= first_in, row <= last_in)
    for a in range(3):
        for g, sy in enumerate((-1, 1)):
            b0 = jnp.where(inside, rim[a][g] * inv_centre[a], 0.0)
            edge_out[g, a, 0:nx + 2, :] = jnp.where(has(0, sy), b0, 0.0)
    for a in range(3):
        for g in range(2):
            y = Y0 + ny if g else Y0 - 1
            for x in range(nx + 2):
                bpad[a, x, y:y + 1, :] = edge_out[g, a, x:x + 1, :]
    apply(bpad, 1, img.at[2])

    def u(a):
        return upad[a, 2:nx + 2, inner, :]

    def z(a):
        return apad[a, 1:nx + 1, inner, :]

    def b(a):
        return bpad[a, 1:nx + 1, inner, :]

    def dot(left, right):
        total = None
        for a in range(3):
            t = left(a) * right(a)
            total = t if total is None else total + t
        return jnp.sum(jnp.sum(total, axis=0), axis=0, keepdims=True)

    red[0:1, :] = dot(lambda a: r0[a], lambda a: own[1, a])
    red[1:2, :] = dot(u, lambda a: img[0, a])
    red[2:3, :] = dot(z, lambda a: img[0, a])
    red[3:4, :] = dot(b, lambda a: img[0, a])
    red[5:6, :] = dot(z, lambda a: img[2, a])
    red[6:7, :] = dot(b, lambda a: img[2, a])
    take(A, 0)
    apply(apad, 1, img.at[1])
    red[4:5, :] = dot(z, lambda a: img[1, a])

    rows = lax.broadcasted_iota(jnp.int32, (8, nz), 0)
    diagonal = rows == lax.broadcasted_iota(jnp.int32, (8, nz), 1)
    each = jnp.sum(red[...], axis=1, keepdims=True)
    red1[...] = jnp.sum(jnp.where(diagonal, each, 0.0), axis=0, keepdims=True)
    n = nd * nb
    me = dom * nb + bud
    rall[me] = red1[...]
    for j in sorted(range(1, n), key=lambda j: abs(2 * j - n)):
        peer = lax.rem(me + j, n)
        remote(red1, rall.at[me], ds.at[0], dr.at[0], peer // nb, lax.rem(peer, nb)).start()

    def every():
        part = rall.at[pl.ds(0, n - 1)]
        return remote(part, part, ds.at[0], dr.at[0], dom, bud)

    start_keep(2, 0)
    start_keep(2, 1)

    take(X, 0)
    apply(xpad, 1, img3)
    centre_value = (HIGH + LOW) / 2.0
    half_width = (HIGH - LOW) / 2.0
    ratio_value = centre_value / half_width
    weight = 1.0 / ratio_value
    for a in range(3):
        t = target[a] - img3[a] * stiff[...]
        d = inv[a] * t / centre_value
        target[a] = t
        update[a] = d
        solved[a] = d
        lpad[a, 1:nx + 1, inner, :] = d * stiff[...]
    for sweep in range(SWEEPS - 1):
        apply(lpad, 1, img3)
        weight_next = 1.0 / (2.0 * ratio_value - weight)
        for a in range(3):
            remain = target[a] - img3[a] * stiff[...]
            d = weight_next * weight * update[a] + (2.0 * weight_next / half_width) * (inv[a] * remain)
            y = solved[a] + d
            update[a] = d
            solved[a] = y
            if sweep < SWEEPS - 2:
                lpad[a, 1:nx + 1, inner, :] = y * stiff[...]
        weight = weight_next

    for a in range(3):
        x_out[a] = jnp.where(me_failed, solved[a], x_in[a])
    s_out[...] = stiff[...]
    for h in (U, A, X):
        end(h)
    for w in range(2):
        for i in range(3):
            for l in range(levels):
                fetch[w][i][l].wait_send()
    for w in range(3):
        for i in range(2):
            for l in range(levels):
                keep[w][i][l].wait_recv()
        for a in range(3):
            got = brecv[0, w, a]
            for l in range(1, levels):
                got = jnp.where(bit_here == l, brecv[l, w, a], got)
            other[w, a] = got

    every().wait_recv()
    total = jnp.sum(rall[...], axis=0)
    sums = jnp.sum(jnp.where(diagonal, jnp.broadcast_to(total, (8, nz)), 0.0), axis=1, keepdims=True)
    g0, c0, e0, f0, h0, h1, h2 = [jnp.broadcast_to(sums[j:j + 1], (1, nz)) for j in range(7)]
    alpha0 = g0 / c0
    g1 = g0 - 2.0 * alpha0 * e0 + alpha0 * alpha0 * f0
    beta0 = g1 / g0
    c1 = (
        h0 - 2.0 * alpha0 * h1 + alpha0 * alpha0 * h2
        + 2.0 * beta0 * (e0 - alpha0 * f0) + beta0 * beta0 * c0
    )
    alpha1 = g1 / c1
    coef[0:1, :] = alpha0
    coef[1:2, :] = beta0
    coef[2:3, :] = alpha1

    for w in range(3):
        for i in range(2):
            for l in range(levels):
                keep[w][i][l].wait_send()
    every().wait_send()


def finish(x0, r0, own, other, img, stiff, coef, x_out, r_out, b_out, xs, rs, bs, sems):
    copies = [pltpu.make_async_copy(other.at[0], b_out.at[0], sems.at[9])]
    copies[0].start()
    alpha0, beta0, alpha1 = coef[0:1, :], coef[1:2, :], coef[2:3, :]
    alpha0, beta0, alpha1 = alpha0[None], beta0[None], alpha1[None]
    for a in range(3):
        bs[a] = other[1, a] - alpha0 * other[2, a] + beta0 * other[0, a]
        p0 = own[0, a]
        p1 = own[1, a] - alpha0 * own[2, a] + beta0 * p0
        xs[a] = x0[a] + alpha0 * p0 + alpha1 * p1
        t0 = img[0, a]
        q1 = img[1, a] - alpha0 * img[2, a] + beta0 * t0
        rs[a] = r0[a] - stiff[...] * (alpha0 * t0 + alpha1 * q1)
        for i, (src, dst) in enumerate((
            (bs.at[a], b_out.at[1, a]), (xs.at[a], x_out.at[a]), (rs.at[a], r_out.at[a]),
        )):
            copies.append(pltpu.make_async_copy(src, dst, sems.at[a * 3 + i]))
            copies[-1].start()
    for c in copies:
        c.wait()


def on_device(nd, nb, rhs, stiff, coupling, x_in, r_in, p_in, backup_in, beta, fc, bb):
    levels = nb.bit_length() - 1
    nx, ny, nz = stiff.shape
    f32 = jnp.float32
    vmem = pl.BlockSpec(memory_space=pltpu.VMEM)
    smem = pl.BlockSpec(memory_space=pltpu.SMEM)
    hbm = pl.BlockSpec(memory_space=pltpu.HBM)
    field = (3, nx, ny, nz)
    dma = pltpu.SemaphoreType.DMA

    def v(*shape):
        return pltpu.VMEM(shape, f32)

    def rim(deep):
        return v(3, nx + 2 * deep, ny + 2 * Y0, nz)

    def strips(deep):
        return [v(2, 3, deep, nx, nz)] * 2 + [v(4, deep, 3, deep, nz)] * 2

    parts = pl.pallas_call(
        functools.partial(kernel, nd, nb, levels),
        out_shape=(
            v(*field), v(*field), v(3, *field), v(3, *field), v(3, *field), v(nx, ny, nz), v(8, nz),
        ),
        in_specs=[hbm] * 7 + [smem] * 3,
        out_specs=(vmem,) * 7,
        scratch_shapes=[
            v(*field), v(nx, ny, nz), pltpu.SMEM((3, 3, 27), f32), v(*field), v(*field), v(*field), v(2, *field),
            dma((7,)),
            rim(2), rim(1), rim(1), rim(1), rim(1),
            *strips(2), *strips(1), *strips(1),
            v(2, 3, 3, nx + 4, nz), v(2, 3, nx + 4, nz), v(levels, 2, *field), v(levels, 3, *field),
            v(*field), v(nx, ny, nz), v(*field), v(*field), v(*field), v(*field),
            v(8, nz), v(1, nz), v(nd * nb, 1, nz),
            *[dma((halo_sems(deep),)) for deep in (2, 1, 1) for _ in range(2)],
            dma((levels, 2, 3)), dma((levels, 2, 3)),
            dma((levels, 3, 2)), dma((levels, 3, 2)),
            dma((1,)), dma((1,)),
            pltpu.SemaphoreType.REGULAR((nd.bit_length(),)),
        ],
        compiler_params=pltpu.CompilerParams(
            collective_id=0, has_side_effects=True, vmem_limit_bytes=40 * 1024 * 1024
        ),
    )(*[pltpu.with_memory_space_constraint(v, pltpu.HBM) for v in (
        rhs, stiff, jnp.transpose(coupling, (1, 2, 0)), x_in, r_in, p_in, backup_in
    )], beta, fc, bb)
    return pl.pallas_call(
        finish,
        out_shape=(
            pltpu.HBM(field, f32), pltpu.HBM(field, f32), pltpu.HBM((2,) + field, f32),
        ),
        in_specs=[vmem] * 7,
        out_specs=(hbm, hbm, hbm),
        scratch_shapes=[
            pltpu.VMEM(field, f32), pltpu.VMEM(field, f32), pltpu.VMEM(field, f32), dma((10,)),
        ],
        compiler_params=pltpu.CompilerParams(vmem_limit_bytes=8 * 1024 * 1024),
    )(*parts)


def solution(mesh):
    nd, nb = mesh.shape["dom"], mesh.shape["bud"]
    placed = (
        P(None, "dom", "bud", None),
        P("dom", "bud", None),
        P(),
        P(None, "dom", "bud", None),
        P(None, "dom", "bud", None),
        P(None, "dom", "bud", None),
        P(None, None, "dom", "bud", None),
        P(),
        P("dom"),
        P("dom"),
    )
    return jax.shard_map(
        functools.partial(on_device, nd, nb),
        mesh=mesh,
        in_specs=placed,
        out_specs=(
            P(None, "dom", "bud", None),
            P(None, "dom", "bud", None),
            P(None, None, "dom", "bud", None),
        ),
        check_vma=False,
    )
```

```python
import functools

import jax
import jax.numpy as jnp
from jax import lax
from jax.experimental import pallas as pl
from jax.experimental.pallas import tpu as pltpu
from jax.sharding import PartitionSpec as P

SWEEPS = 4
LOW = 0.01
HIGH = 1.99
Y0 = 8
CORNERS = [(sx, sy) for sx in (-1, 1) for sy in (-1, 1)]


class Halo:
    def __init__(self, depth, pad, ysend, yrecv, csend, crecv, recv, zero):
        self.depth, self.pad = depth, pad
        self.ysend, self.yrecv, self.csend, self.crecv = ysend, yrecv, csend, crecv
        self.recv, self.zero = recv, zero


def halo_rows(nx, ny, depth):
    return 6 * ny + 6 * depth * nx + 12 * depth


def kernel(
    nd, nb, levels,
    rhs_h, stiff_h, cpl_h, x_h, r_h, p_h, bk_h, beta, fc, bb,
    x_out, r0, own, other, img, s_out, coef,
    rhs, stiff, cpl, x_in, r_in, p_in, bk, in_sems,
    upad, apad, xpad, bpad, lpad,
    yus, yur, cus, cur, yas, yar, cas, car, yxs, yxr, cxs, cxr,
    edge, edge_out, saved, brecv,
    inv, invs, img3, target, solved, update,
    red, red1, rall,
    zx, zy2, zy1, zc2, zc1, dummy,
    hs, ur, ar, xr, ss, sr, bs, br, ds, dr, know,
):
    nx, ny, nz = stiff.shape
    step = 2 if nx % 2 == 0 else 1
    dom, bud = lax.axis_index("dom"), lax.axis_index("bud")
    f32 = jnp.float32

    def has(sx, sy):
        ok = None
        for cond in (
            ([dom > 0] if sx < 0 else [dom < nd - 1] if sx > 0 else [])
            + ([bud > 0] if sy < 0 else [bud < nb - 1] if sy > 0 else [])
        ):
            ok = cond if ok is None else jnp.logical_and(ok, cond)
        return ok

    def remote(src, dst, send, recv, d, b):
        return pltpu.make_async_remote_copy(
            src_ref=src, dst_ref=dst, send_sem=send, recv_sem=recv,
            device_id={"dom": d, "bud": b}, device_id_type=pl.DeviceIdType.MESH,
        )

    def flip(level):
        stride = 1 << level
        return bud + stride * (1 - 2 * (lax.rem(bud // stride, 2)))

    barrier = pltpu.get_barrier_semaphore()

    def greet(sem, d, b):
        pl.semaphore_signal(
            sem, inc=1, device_id={"dom": d, "bud": b},
            device_id_type=pl.DeviceIdType.MESH,
        )

    def ahead(stride):
        return jnp.where(dom >= stride, 1, 0) + jnp.where(dom < nd - stride, 1, 0)

    def greet_dom(sem, stride):
        @pl.when(dom >= stride)
        def _():
            greet(sem, dom - stride, bud)

        @pl.when(dom < nd - stride)
        def _():
            greet(sem, dom + stride, bud)

    def greet_near(sem):
        greet_dom(sem, 1)
        for j in range(1, nb):
            greet(sem, dom, lax.rem(bud + j, nb))

    strides = [1 << i for i in range(max(nd - 1, 1).bit_length())]
    greet_near(barrier)

    loads = {}
    for i, (name, src, dst) in enumerate((
        ("cpl", cpl_h, cpl), ("bk", bk_h, bk), ("stiff", stiff_h, stiff), ("x", x_h, x_in),
        ("p", p_h, p_in), ("r", r_h, r_in), ("rhs", rhs_h, rhs),
    )):
        loads[name] = pltpu.make_async_copy(src, dst, in_sems.at[i])
        loads[name].start()

    for zero in (zx, zy2, zy1, zc2, zc1):
        zero[...] = jnp.zeros(zero.shape, f32)
    U = Halo(2, upad, yus, yur, cus, cur, ur, (zx, zy2, zc2))
    A = Halo(1, apad, yas, yar, cas, car, ar, (zx, zy1, zc1))
    X = Halo(1, xpad, yxs, yxr, cxs, cxr, xr, (zx, zy1, zc1))
    inner = pl.ds(Y0, ny)

    def either(sx, sy, there, beyond):
        @pl.when(has(sx, sy))
        def _():
            there().start()

        @pl.when(jnp.logical_not(has(sx, sy)))
        def _():
            beyond().start()

    def send_x(h, sx, d):
        deep = h.depth
        low, high = deep - 1 - d, deep + nx + d
        src = deep + (nx - 1 - d if sx > 0 else d)
        to, own_side = (low, high) if sx > 0 else (high, low)
        either(sx, 0, lambda: remote(
            h.pad.at[:, src, inner, :], h.pad.at[:, to, inner, :], hs.at[1 if sx > 0 else 0], h.recv.at[d],
            dom + sx, bud,
        ), lambda: pltpu.make_async_copy(h.zero[0], h.pad.at[:, own_side, inner, :], h.recv.at[d]))

    def send_y(h, sy):
        i = 1 if sy > 0 else 0
        either(0, sy, lambda: remote(
            h.ysend.at[i], h.yrecv.at[1 - i], hs.at[2 + i], h.recv.at[0], dom, bud + sy,
        ), lambda: pltpu.make_async_copy(h.zero[1], h.yrecv.at[i], h.recv.at[0]))

    def send_c(h, q, e):
        sx, sy = CORNERS[q]
        either(sx, sy, lambda: remote(
            h.csend.at[q, e], h.crecv.at[3 - q, e], hs.at[4 + q], h.recv.at[e], dom + sx, bud + sy,
        ), lambda: pltpu.make_async_copy(h.zero[2], h.crecv.at[q, e], h.recv.at[e]))

    def send_xc(h, sx, d):
        for q in range(4):
            if CORNERS[q][0] == sx:
                pack_c(h, q, d)
        for q in range(4):
            if CORNERS[q][0] == sx:
                send_c(h, q, d)
        send_x(h, sx, d)

    def end_halos():
        deeps = (2, 1, 1)
        for i, (sx, sy, rows) in enumerate(
            [(sx, 0, 3 * ny * sum(deeps)) for sx in (-1, 1)]
            + [(0, sy, 3 * nx * sum(deeps)) for sy in (-1, 1)]
            + [(sx, sy, 3 * sum(d * d for d in deeps)) for sx, sy in CORNERS]
        ):
            @pl.when(has(sx, sy))
            def _(i=i, sx=sx, sy=sy, rows=rows):
                part = dummy.at[pl.ds(0, rows)]
                remote(part, part, hs.at[i], hs.at[i], dom + sx, bud + sy).wait_send()

    def pack_y(h):
        deep = h.depth
        for i in range(2):
            for b in range(3):
                for d in range(deep):
                    y = Y0 + (ny - deep + d if i else d)
                    for x in range(nx):
                        h.ysend[i, b, d, x:x + 1, :] = h.pad[b, deep + x, y:y + 1, :]

    def pack_c(h, q, e):
        deep = h.depth
        sx, sy = CORNERS[q]
        x = deep + (nx - 1 - e if sx > 0 else e)
        for b in range(3):
            for d in range(deep):
                y = Y0 + (ny - deep + d if sy > 0 else d)
                h.csend[q, e, b, d:d + 1, :] = h.pad[b, x, y:y + 1, :]

    def unpack_y(h):
        deep = h.depth
        for i in range(2):
            y, d = (Y0 + ny, 0) if i else (Y0 - 1, deep - 1)
            for b in range(3):
                for x in range(nx):
                    h.pad[b, deep + x, y:y + 1, :] = h.yrecv[i, b, d, x:x + 1, :]

    def unpack_c(h, e):
        deep = h.depth
        for q, (sx, sy) in enumerate(CORNERS):
            x = deep + nx + e if sx > 0 else deep - 1 - e
            y, d = (Y0 + ny, 0) if sy > 0 else (Y0 - 1, deep - 1)
            for b in range(3):
                h.pad[b, x, y:y + 1, :] = h.crecv[q, e, b, d:d + 1, :]

    def take(h, d):
        rows = 6 * ny + 12 * h.depth + (6 * h.depth * nx if d == 0 else 0)
        part = dummy.at[pl.ds(0, rows)]
        pltpu.make_async_copy(part, part, h.recv.at[d]).wait()
        if d == 0:
            unpack_y(h)
        unpack_c(h, d)

    def stencil(load, groups):
        acc = [[[None] * groups for _ in range(3)] for _ in range(3)]
        for dx in range(3):
            for dy in range(3):
                for b in range(3):
                    ws = [load(b, dx, dy, g) for g in range(groups)]
                    for dz in range(3):
                        o = (dx * 3 + dy) * 3 + dz
                        for a in range(3):
                            for g in range(groups):
                                term = cpl[a, b, o] * ws[g]
                                old = acc[dz][a][g]
                                acc[dz][a][g] = term if old is None else old + term
        lane = lax.broadcasted_iota(jnp.int32, acc[0][0][0].shape, 1)

        def joined(a, g):
            before = jnp.where(lane == 0, 0.0, pltpu.roll(acc[0][a][g], 1, 1))
            after = jnp.where(lane == nz - 1, 0.0, pltpu.roll(acc[2][a][g], nz - 1, 1))
            return acc[1][a][g] + before + after

        return [[joined(a, g) for g in range(groups)] for a in range(3)]

    def apply(pad, deep, out):
        @pl.loop(0, nx // step)
        def _(j):
            x = j * step
            got = stencil(
                lambda b, dx, dy, g: pad[b, x + (g + deep - 1 + dx), Y0 - 1 + dy:Y0 - 1 + dy + ny, :], step
            )
            for a in range(3):
                for g in range(step):
                    out[a, x + g] = got[a][g]

    for name in ("cpl", "stiff", "x", "bk"):
        loads[name].wait()
    me_failed = jnp.full((1, ny, nz), fc[0], jnp.int32) == bud
    bit_here = jnp.full((1, ny, nz), bb[0], jnp.int32)
    centre = [cpl[a, a, 13] for a in range(3)]
    for a in range(3):
        xpad[a, 1:nx + 1, inner, :] = jnp.where(me_failed, 0.0, x_in[a] * stiff[...])
    pack_y(X)

    pl.semaphore_wait(barrier, nb - 1 + ahead(1))

    order = [slice(x, x + 1) for x in (0, nx - 1, 1, nx - 2)] + ([slice(2, nx - 2)] if nx > 4 else [])
    for w in (1, 0):
        for i, x in enumerate(order):
            x = pl.ds(x.start, x.stop - x.start)
            for l in range(levels):
                remote(
                    bk.at[w, :, x], saved.at[l, w, :, x], ss.at[0], sr.at[w, i], dom, flip(l)
                ).start()

    def fetched(w, i):
        x = order[i]
        part = saved.at[:, w, :, pl.ds(x.start, x.stop - x.start)]
        pltpu.make_async_copy(part, part, sr.at[w, i]).wait()

    greet_near(know.at[0])
    for sx in (-1, 1):
        send_x(X, sx, 0)
    for sy in (-1, 1):
        send_y(X, sy)

    coef[...] = jnp.zeros(coef.shape, f32)
    red[...] = jnp.zeros(red.shape, f32)
    for x in (0, nx + 1):
        lpad[:, x] = jnp.zeros((3, ny + 2 * Y0, nz), f32)
    for y in (0, Y0 + ny):
        lpad[:, 1:nx + 1, y:y + Y0, :] = jnp.zeros((3, nx, Y0, nz), f32)
    invs[...] = 1.0 / stiff[...]
    inv_centre = [1.0 / jnp.full((1, nz), centre[a], f32) for a in range(3)]
    for a in range(3):
        inv[a] = 1.0 / (stiff[...] * stiff[...] * centre[a])

    pl.semaphore_wait(know.at[0], nb - 1 + ahead(1))
    if len(strides) > 1:
        greet_dom(know.at[1], strides[1])
    for q in range(4):
        pack_c(X, q, 0)
    for q in range(4):
        send_c(X, q, 0)

    def pick(value, l_of):
        got = l_of(0)
        for l in range(1, levels):
            got = jnp.where(bit_here == l, l_of(l), got)
        return jnp.where(me_failed, got, value)

    def start_field(x):
        for a in range(3):
            p0 = pick(p_in[a, x], lambda l: saved[l, 1, a, x])
            own[0, a, x] = p0
            upad[a, x.start + 2:x.stop + 2, inner, :] = p0 * stiff[x]

    loads["p"].wait()
    for i, x in enumerate(order):
        fetched(1, i)
        start_field(x)
        if i < 4:
            send_xc(U, (-1, 1)[i % 2], i // 2)
    pack_y(U)
    for sy in (-1, 1):
        send_y(U, sy)

    def start_keep(w, x):
        for l in range(levels):
            remote(own.at[w, :, x], brecv.at[l, w, :, x], bs.at[0], br.at[0], dom, flip(l)).start()

    start_keep(0, pl.ds(0, nx - 1))
    for i in range(1, len(strides)):
        pl.semaphore_wait(know.at[i], ahead(strides[i]))
        if i + 1 < len(strides):
            greet_dom(know.at[i + 1], strides[i + 1])

    def second_field(x):
        for a in range(3):
            s = stiff[x]
            restored_z = pick(0.0, lambda l: saved[l, 1, a, x]) - beta[0] * pick(0.0, lambda l: saved[l, 0, a, x])
            restored_r = restored_z * (s * s * centre[a])
            z0 = jnp.where(me_failed, restored_z, inv[a, x] * r_in[a, x])
            r0[a, x] = jnp.where(me_failed, restored_r, r_in[a, x])
            target[a, x] = rhs[a, x] - restored_r
            own[1, a, x] = z0
            apad[a, x.start + 1:x.stop + 1, inner, :] = z0 * s

    for name in ("r", "rhs"):
        loads[name].wait()
    for i, x in enumerate(order):
        fetched(0, i)
        second_field(x)
        if i < 2:
            send_xc(A, (-1, 1)[i], 0)
    pack_y(A)
    for sy in (-1, 1):
        send_y(A, sy)
    start_keep(0, pl.ds(nx - 1, 1))
    start_keep(1, pl.ds(0, nx))

    take(U, 0)
    apply(upad, 2, img.at[0])
    for a in range(3):
        b0 = img[0, a] * inv_centre[a]
        bpad[a, 1:nx + 1, inner, :] = b0
        own[2, a] = b0 * invs[...]
    take(U, 1)
    for b in range(3):
        for i in range(2):
            for d in range(2):
                lev = i + d
                edge[i, b, lev, 2:nx + 2, :] = yur[i, b, d]
                for q, (sx, sy) in enumerate(CORNERS):
                    if (sy > 0) == bool(i):
                        for e in range(2):
                            x = nx + 2 + e if sx > 0 else 1 - e
                            edge[i, b, lev, x:x + 1, :] = cur[q, e, b, d:d + 1, :]
            y = Y0 + (ny - 1 if i else 0)
            for x in range(nx + 4):
                edge[i, b, 0 if i else 2, x:x + 1, :] = upad[b, x, y:y + 1, :]

    rim = stencil(lambda b, dx, dy, g: upad[b, (nx + 1 if g else 0) + dx, Y0 - 1 + dy:Y0 - 1 + dy + ny, :], 2)
    for a in range(3):
        for g, sx in enumerate((-1, 1)):
            b0 = rim[a][g] * inv_centre[a]
            bpad[a, nx + 1 if g else 0, inner, :] = jnp.where(has(sx, 0), b0, 0.0)
    rim = stencil(lambda b, dx, dy, g: edge[g, b, dy, dx:dx + nx + 2, :], 2)
    row = lax.broadcasted_iota(jnp.int32, (nx + 2, nz), 0)
    first_in = jnp.where(dom > 0, 0, 1)
    last_in = jnp.where(dom < nd - 1, nx + 1, nx)
    inside = jnp.logical_and(row >= first_in, row <= last_in)
    for a in range(3):
        for g, sy in enumerate((-1, 1)):
            b0 = jnp.where(inside, rim[a][g] * inv_centre[a], 0.0)
            edge_out[g, a, 0:nx + 2, :] = jnp.where(has(0, sy), b0, 0.0)
    for a in range(3):
        for g in range(2):
            y = Y0 + ny if g else Y0 - 1
            for x in range(nx + 2):
                bpad[a, x, y:y + 1, :] = edge_out[g, a, x:x + 1, :]
    apply(bpad, 1, img.at[2])

    def u(a):
        return upad[a, 2:nx + 2, inner, :]

    def z(a):
        return apad[a, 1:nx + 1, inner, :]

    def b(a):
        return bpad[a, 1:nx + 1, inner, :]

    def dot(left, right):
        total = None
        for a in range(3):
            t = left(a) * right(a)
            total = t if total is None else total + t
        return jnp.sum(jnp.sum(total, axis=0), axis=0, keepdims=True)

    red[0:1, :] = dot(lambda a: r0[a], lambda a: own[1, a])
    red[1:2, :] = dot(u, lambda a: img[0, a])
    red[2:3, :] = dot(z, lambda a: img[0, a])
    red[3:4, :] = dot(b, lambda a: img[0, a])
    red[5:6, :] = dot(z, lambda a: img[2, a])
    red[6:7, :] = dot(b, lambda a: img[2, a])
    take(A, 0)
    apply(apad, 1, img.at[1])
    red[4:5, :] = dot(z, lambda a: img[1, a])

    rows = lax.broadcasted_iota(jnp.int32, (8, nz), 0)
    diagonal = rows == lax.broadcasted_iota(jnp.int32, (8, nz), 1)
    each = jnp.sum(red[...], axis=1, keepdims=True)
    red1[...] = jnp.sum(jnp.where(diagonal, each, 0.0), axis=0, keepdims=True)
    n = nd * nb
    me = dom * nb + bud
    rall[me] = red1[...]
    bits = [(1 << i) * (1 - 2 * lax.rem(dom // (1 << i), 2)) for i in range((nd - 1).bit_length())]
    for mask in range(nd - 1, -1, -1):
        to = dom + sum(bit for i, bit in enumerate(bits) if mask >> i & 1)
        for j in range(nb):
            if mask or j:
                remote(red1, rall.at[me], ds.at[0], dr.at[0], to, lax.rem(bud + j, nb)).start()

    def every():
        part = rall.at[pl.ds(0, n - 1)]
        return remote(part, part, ds.at[0], dr.at[0], dom, bud)

    start_keep(2, pl.ds(0, nx))

    take(X, 0)
    apply(xpad, 1, img3)
    centre_value = (HIGH + LOW) / 2.0
    half_width = (HIGH - LOW) / 2.0
    ratio_value = centre_value / half_width
    weight = 1.0 / ratio_value
    for a in range(3):
        t = target[a] - img3[a] * stiff[...]
        d = inv[a] * t / centre_value
        target[a] = t
        update[a] = d
        solved[a] = d
        lpad[a, 1:nx + 1, inner, :] = d * stiff[...]
    for sweep in range(SWEEPS - 1):
        apply(lpad, 1, img3)
        weight_next = 1.0 / (2.0 * ratio_value - weight)
        for a in range(3):
            remain = target[a] - img3[a] * stiff[...]
            d = weight_next * weight * update[a] + (2.0 * weight_next / half_width) * (inv[a] * remain)
            y = solved[a] + d
            update[a] = d
            solved[a] = y
            if sweep < SWEEPS - 2:
                lpad[a, 1:nx + 1, inner, :] = y * stiff[...]
        weight = weight_next

    for a in range(3):
        x_out[a] = jnp.where(me_failed, solved[a], x_in[a])
    s_out[...] = stiff[...]
    end_halos()

    def all_of(ref, sem):
        return remote(ref, ref, sem.at[0], sem.at[0], dom, bud)

    all_of(saved, ss).wait_send()
    all_of(brecv, bs).wait_send()
    every().wait_send()
    pltpu.make_async_copy(brecv, brecv, br.at[0]).wait()
    for w in range(3):
        for a in range(3):
            got = brecv[0, w, a]
            for l in range(1, levels):
                got = jnp.where(bit_here == l, brecv[l, w, a], got)
            other[w, a] = got

    every().wait_recv()
    total = jnp.sum(rall[...], axis=0)
    sums = jnp.sum(jnp.where(diagonal, jnp.broadcast_to(total, (8, nz)), 0.0), axis=1, keepdims=True)
    g0, c0, e0, f0, h0, h1, h2 = [jnp.broadcast_to(sums[j:j + 1], (1, nz)) for j in range(7)]
    alpha0 = g0 / c0
    g1 = g0 - 2.0 * alpha0 * e0 + alpha0 * alpha0 * f0
    beta0 = g1 / g0
    c1 = (
        h0 - 2.0 * alpha0 * h1 + alpha0 * alpha0 * h2
        + 2.0 * beta0 * (e0 - alpha0 * f0) + beta0 * beta0 * c0
    )
    alpha1 = g1 / c1
    coef[0:1, :] = alpha0
    coef[1:2, :] = beta0
    coef[2:3, :] = alpha1


def finish(x0, r0, own, other, img, stiff, coef, x_out, r_out, b_out, xs, rs, bs, sems):
    copies = [pltpu.make_async_copy(other.at[0], b_out.at[0], sems.at[9])]
    copies[0].start()
    alpha0, beta0, alpha1 = coef[0:1, :], coef[1:2, :], coef[2:3, :]
    alpha0, beta0, alpha1 = alpha0[None], beta0[None], alpha1[None]
    for a in range(3):
        bs[a] = other[1, a] - alpha0 * other[2, a] + beta0 * other[0, a]
        p0 = own[0, a]
        p1 = own[1, a] - alpha0 * own[2, a] + beta0 * p0
        xs[a] = x0[a] + alpha0 * p0 + alpha1 * p1
        t0 = img[0, a]
        q1 = img[1, a] - alpha0 * img[2, a] + beta0 * t0
        rs[a] = r0[a] - stiff[...] * (alpha0 * t0 + alpha1 * q1)
        for i, (src, dst) in enumerate((
            (bs.at[a], b_out.at[1, a]), (xs.at[a], x_out.at[a]), (rs.at[a], r_out.at[a]),
        )):
            copies.append(pltpu.make_async_copy(src, dst, sems.at[a * 3 + i]))
            copies[-1].start()
    for c in copies:
        c.wait()


def on_device(nd, nb, rhs, stiff, coupling, x_in, r_in, p_in, backup_in, beta, fc, bb):
    levels = nb.bit_length() - 1
    nx, ny, nz = stiff.shape
    f32 = jnp.float32
    vmem = pl.BlockSpec(memory_space=pltpu.VMEM)
    smem = pl.BlockSpec(memory_space=pltpu.SMEM)
    hbm = pl.BlockSpec(memory_space=pltpu.HBM)
    field = (3, nx, ny, nz)
    dma = pltpu.SemaphoreType.DMA

    def v(*shape):
        return pltpu.VMEM(shape, f32)

    def rim(deep):
        return v(3, nx + 2 * deep, ny + 2 * Y0, nz)

    def strips(deep):
        return [v(2, 3, deep, nx, nz)] * 2 + [v(4, deep, 3, deep, nz)] * 2

    parts = pl.pallas_call(
        functools.partial(kernel, nd, nb, levels),
        out_shape=(
            v(*field), v(*field), v(3, *field), v(3, *field), v(3, *field), v(nx, ny, nz), v(8, nz),
        ),
        in_specs=[hbm] * 7 + [smem] * 3,
        out_specs=(vmem,) * 7,
        scratch_shapes=[
            v(*field), v(nx, ny, nz), pltpu.SMEM((3, 3, 27), f32), v(*field), v(*field), v(*field), v(2, *field),
            dma((7,)),
            rim(2), rim(1), rim(1), rim(1), rim(1),
            *strips(2), *strips(1), *strips(1),
            v(2, 3, 3, nx + 4, nz), v(2, 3, nx + 4, nz), v(levels, 2, *field), v(levels, 3, *field),
            v(*field), v(nx, ny, nz), v(*field), v(*field), v(*field), v(*field),
            v(8, nz), v(1, nz), v(nd * nb, 1, nz),
            v(3, ny, nz), v(3, 2, nx, nz), v(3, 1, nx, nz), v(3, 2, nz), v(3, 1, nz),
            v(max(12 * ny, halo_rows(nx, ny, 2)), 1, nz),
            dma((8,)), dma((2,)), dma((1,)), dma((1,)),
            dma((1,)), dma((2, 4 if nx == 4 else 5)),
            dma((1,)), dma((1,)), dma((1,)), dma((1,)),
            pltpu.SemaphoreType.REGULAR((max((nd - 1).bit_length(), 1),)),
        ],
        compiler_params=pltpu.CompilerParams(
            collective_id=0, has_side_effects=True, vmem_limit_bytes=40 * 1024 * 1024
        ),
    )(*[pltpu.with_memory_space_constraint(v, pltpu.HBM) for v in (
        rhs, stiff, jnp.transpose(coupling, (1, 2, 0)), x_in, r_in, p_in, backup_in
    )], beta, fc, bb)
    return pl.pallas_call(
        finish,
        out_shape=(
            pltpu.HBM(field, f32), pltpu.HBM(field, f32), pltpu.HBM((2,) + field, f32),
        ),
        in_specs=[vmem] * 7,
        out_specs=(hbm, hbm, hbm),
        scratch_shapes=[
            pltpu.VMEM(field, f32), pltpu.VMEM(field, f32), pltpu.VMEM(field, f32), dma((10,)),
        ],
        compiler_params=pltpu.CompilerParams(vmem_limit_bytes=8 * 1024 * 1024),
    )(*parts)


def solution(mesh):
    nd, nb = mesh.shape["dom"], mesh.shape["bud"]
    placed = (
        P(None, "dom", "bud", None),
        P("dom", "bud", None),
        P(),
        P(None, "dom", "bud", None),
        P(None, "dom", "bud", None),
        P(None, "dom", "bud", None),
        P(None, None, "dom", "bud", None),
        P(),
        P("dom"),
        P("dom"),
    )
    return jax.shard_map(
        functools.partial(on_device, nd, nb),
        mesh=mesh,
        in_specs=placed,
        out_specs=(
            P(None, "dom", "bud", None),
            P(None, "dom", "bud", None),
            P(None, None, "dom", "bud", None),
        ),
        check_vma=False,
    )
```

```python
import functools

import jax
import jax.numpy as jnp
from jax import lax
from jax.experimental import pallas as pl
from jax.experimental.pallas import tpu as pltpu
from jax.sharding import PartitionSpec as P

SWEEPS = 4
LOW = 0.01
HIGH = 1.99
Y0 = 8
CORNERS = [(sx, sy) for sx in (-1, 1) for sy in (-1, 1)]


class Halo:
    def __init__(self, depth, pad, ysend, yrecv, csend, crecv, recv, zero):
        self.depth, self.pad = depth, pad
        self.ysend, self.yrecv, self.csend, self.crecv = ysend, yrecv, csend, crecv
        self.recv, self.zero = recv, zero


def halo_rows(nx, ny, depth):
    return 6 * ny + 6 * depth * nx + 12 * depth


def kernel(
    nd, nb, levels,
    rhs_h, stiff_h, cpl_h, x_h, r_h, p_h, bk_h, beta, fc, bb,
    x_out, r0, own, other, img, s_out, coef,
    rhs, stiff, cpl, x_in, r_in, p_in, bk, in_sems,
    upad, apad, xpad, bpad, lpad,
    yus, yur, cus, cur, yas, yar, cas, car, yxs, yxr, cxs, cxr,
    edge, urim, arim, brim, ytmp, saved, brecv,
    inv, invs, img3, target, solved, update,
    red, red1, rall,
    zx, zy2, zy1, zc2, zc1, dummy,
    hs, ur, ar, xr, ss, sr, bs, br, ds, dr, know,
):
    nx, ny, nz = stiff.shape
    step = 2 if nx % 2 == 0 else 1
    dom, bud = lax.axis_index("dom"), lax.axis_index("bud")
    f32 = jnp.float32

    def has(sx, sy):
        ok = None
        for cond in (
            ([dom > 0] if sx < 0 else [dom < nd - 1] if sx > 0 else [])
            + ([bud > 0] if sy < 0 else [bud < nb - 1] if sy > 0 else [])
        ):
            ok = cond if ok is None else jnp.logical_and(ok, cond)
        return ok

    def remote(src, dst, send, recv, d, b):
        return pltpu.make_async_remote_copy(
            src_ref=src, dst_ref=dst, send_sem=send, recv_sem=recv,
            device_id={"dom": d, "bud": b}, device_id_type=pl.DeviceIdType.MESH,
        )

    def flip(level):
        stride = 1 << level
        return bud + stride * (1 - 2 * (lax.rem(bud // stride, 2)))

    barrier = pltpu.get_barrier_semaphore()

    def greet(sem, d, b):
        pl.semaphore_signal(
            sem, inc=1, device_id={"dom": d, "bud": b},
            device_id_type=pl.DeviceIdType.MESH,
        )

    def ahead(stride):
        return jnp.where(dom >= stride, 1, 0) + jnp.where(dom < nd - stride, 1, 0)

    def greet_dom(sem, stride):
        @pl.when(dom >= stride)
        def _():
            greet(sem, dom - stride, bud)

        @pl.when(dom < nd - stride)
        def _():
            greet(sem, dom + stride, bud)

    def greet_near(sem):
        greet_dom(sem, 1)
        for j in range(1, nb):
            greet(sem, dom, lax.rem(bud + j, nb))

    strides = [1 << i for i in range(max(nd - 1, 1).bit_length())]
    greet_near(barrier)

    loads = {}
    for i, (name, src, dst) in enumerate((
        ("cpl", cpl_h, cpl), ("bk", bk_h, bk), ("stiff", stiff_h, stiff), ("x", x_h, x_in),
        ("p", p_h, p_in), ("r", r_h, r_in), ("rhs", rhs_h, rhs),
    )):
        loads[name] = pltpu.make_async_copy(src, dst, in_sems.at[i])
        loads[name].start()

    for zero in (zx, zy2, zy1, zc2, zc1):
        zero[...] = jnp.zeros(zero.shape, f32)
    U = Halo(2, upad, yus, yur, cus, cur, ur, (zx, zy2, zc2))
    A = Halo(1, apad, yas, yar, cas, car, ar, (zx, zy1, zc1))
    X = Halo(1, xpad, yxs, yxr, cxs, cxr, xr, (zx, zy1, zc1))
    inner = pl.ds(Y0, ny)

    def either(sx, sy, there, beyond):
        @pl.when(has(sx, sy))
        def _():
            there().start()

        @pl.when(jnp.logical_not(has(sx, sy)))
        def _():
            beyond().start()

    def send_x(h, sx, d):
        deep = h.depth
        low, high = deep - 1 - d, deep + nx + d
        src = deep + (nx - 1 - d if sx > 0 else d)
        to, own_side = (low, high) if sx > 0 else (high, low)
        either(sx, 0, lambda: remote(
            h.pad.at[:, src, inner, :], h.pad.at[:, to, inner, :], hs.at[1 if sx > 0 else 0], h.recv.at[d],
            dom + sx, bud,
        ), lambda: pltpu.make_async_copy(h.zero[0], h.pad.at[:, own_side, inner, :], h.recv.at[d]))

    def send_y(h, sy):
        i = 1 if sy > 0 else 0
        either(0, sy, lambda: remote(
            h.ysend.at[i], h.yrecv.at[1 - i], hs.at[2 + i], h.recv.at[0], dom, bud + sy,
        ), lambda: pltpu.make_async_copy(h.zero[1], h.yrecv.at[i], h.recv.at[0]))

    def send_c(h, q, e):
        sx, sy = CORNERS[q]
        either(sx, sy, lambda: remote(
            h.csend.at[q, e], h.crecv.at[3 - q, e], hs.at[4 + q], h.recv.at[e], dom + sx, bud + sy,
        ), lambda: pltpu.make_async_copy(h.zero[2], h.crecv.at[q, e], h.recv.at[e]))

    def send_xc(h, sx, d):
        for q in range(4):
            if CORNERS[q][0] == sx:
                pack_c(h, q, d)
        for q in range(4):
            if CORNERS[q][0] == sx:
                send_c(h, q, d)
        send_x(h, sx, d)

    def end_halos():
        deeps = (2, 1, 1)
        for i, (sx, sy, rows) in enumerate(
            [(sx, 0, 3 * ny * sum(deeps)) for sx in (-1, 1)]
            + [(0, sy, 3 * nx * sum(deeps)) for sy in (-1, 1)]
            + [(sx, sy, 3 * sum(d * d for d in deeps)) for sx, sy in CORNERS]
        ):
            @pl.when(has(sx, sy))
            def _(i=i, sx=sx, sy=sy, rows=rows):
                part = dummy.at[pl.ds(0, rows)]
                remote(part, part, hs.at[i], hs.at[i], dom + sx, bud + sy).wait_send()

    def pack_y(h):
        deep = h.depth
        for i in range(2):
            for b in range(3):
                for d in range(deep):
                    y = Y0 + (ny - deep + d if i else d)
                    for x in range(nx):
                        h.ysend[i, b, d, x:x + 1, :] = h.pad[b, deep + x, y:y + 1, :]

    def pack_c(h, q, e):
        deep = h.depth
        sx, sy = CORNERS[q]
        x = deep + (nx - 1 - e if sx > 0 else e)
        for b in range(3):
            for d in range(deep):
                y = Y0 + (ny - deep + d if sy > 0 else d)
                h.csend[q, e, b, d:d + 1, :] = h.pad[b, x, y:y + 1, :]

    def unpack_y(h, xs):
        deep = h.depth
        for i in range(2):
            y, d = (Y0 + ny, 0) if i else (Y0 - 1, deep - 1)
            for b in range(3):
                for x in xs:
                    h.pad[b, deep + x, y:y + 1, :] = h.yrecv[i, b, d, x:x + 1, :]

    def unpack_c(h, e):
        deep = h.depth
        for q, (sx, sy) in enumerate(CORNERS):
            x = deep + nx + e if sx > 0 else deep - 1 - e
            y, d = (Y0 + ny, 0) if sy > 0 else (Y0 - 1, deep - 1)
            for b in range(3):
                h.pad[b, x, y:y + 1, :] = h.crecv[q, e, b, d:d + 1, :]

    def take(h, d):
        rows = 6 * ny + 12 * h.depth + (6 * h.depth * nx if d == 0 else 0)
        part = dummy.at[pl.ds(0, rows)]
        pltpu.make_async_copy(part, part, h.recv.at[d]).wait()
        unpack_c(h, d)

    def stencil(load, groups):
        acc = [[[None] * groups for _ in range(3)] for _ in range(3)]
        for dx in range(3):
            for dy in range(3):
                for b in range(3):
                    ws = [load(b, dx, dy, g) for g in range(groups)]
                    if all(w is None for w in ws):
                        continue
                    for dz in range(3):
                        o = (dx * 3 + dy) * 3 + dz
                        for a in range(3):
                            for g in range(groups):
                                if ws[g] is None:
                                    continue
                                term = cpl[a, b, o] * ws[g]
                                old = acc[dz][a][g]
                                acc[dz][a][g] = term if old is None else old + term
        lane = lax.broadcasted_iota(jnp.int32, acc[0][0][0].shape, 1)

        def joined(a, g):
            before = jnp.where(lane == 0, 0.0, pltpu.roll(acc[0][a][g], 1, 1))
            after = jnp.where(lane == nz - 1, 0.0, pltpu.roll(acc[2][a][g], nz - 1, 1))
            return acc[1][a][g] + before + after

        return [[joined(a, g) for g in range(groups)] for a in range(3)]

    def apply(pad, deep, out):
        @pl.loop(0, nx // step)
        def _(j):
            x = j * step
            got = stencil(
                lambda b, dx, dy, g: pad[b, x + (g + deep - 1 + dx), Y0 - 1 + dy:Y0 - 1 + dy + ny, :], step
            )
            for a in range(3):
                for g in range(step):
                    out[a, x + g] = got[a][g]

    def from_own(pad, deep, out):
        for x in range(0, nx, step):
            got = stencil(
                lambda b, dx, dy, g: pad[b, x + g + deep - 1 + dx, Y0 - 1 + dy:Y0 - 1 + dy + ny, :]
                if 0 <= x + g + dx - 1 < nx else None, step
            )
            for a in range(3):
                for g in range(step):
                    out[a, x + g] = got[a][g]

    def from_row(pad, deep, out, source, touched):
        targets = [x for x in (source - 1, source, source + 1) if 0 <= x < nx]
        for xs in (targets[:2], targets[2:]):
            if not xs:
                continue
            got = stencil(
                lambda b, dx, dy, g: pad[b, source + deep, Y0 - 1 + dy:Y0 - 1 + dy + ny, :]
                if dx == source - xs[g] + 1 else None, len(xs)
            )
            for a in range(3):
                for g, x in enumerate(xs):
                    out[a, x] = out[a, x] + got[a][g] if x in touched else got[a][g]
            touched.update(xs)

    def from_rim(pad, deep, strip, out):
        got = stencil(
            lambda b, dx, dy, g: strip[g, b, dx:dx + nx, :] if dy == 2 * g else None, 2
        )
        for a in range(3):
            for g in range(2):
                ytmp[g, a, 0:nx, :] = got[a][g]
        got = stencil(
            lambda b, dx, dy, g: pad[b, deep + nx if g else deep - 1, Y0 - 1 + dy:Y0 - 1 + dy + ny, :]
            if dx == 2 * g else None, 2
        )
        for a in range(3):
            for g, x in enumerate((0, nx - 1)):
                out[a, x] = out[a, x] + got[a][g]
        for a in range(3):
            for g, y in enumerate((0, ny - 1)):
                for x in range(nx):
                    out[a, x, y:y + 1, :] = out[a, x, y:y + 1, :] + ytmp[g, a, x:x + 1, :]

    for name in ("cpl", "stiff", "x", "bk"):
        loads[name].wait()
    me_failed = jnp.full((1, ny, nz), fc[0], jnp.int32) == bud
    bit_here = jnp.full((1, ny, nz), bb[0], jnp.int32)
    centre = [cpl[a, a, 13] for a in range(3)]
    for a in range(3):
        xpad[a, 1:nx + 1, inner, :] = jnp.where(me_failed, 0.0, x_in[a] * stiff[...])
    pack_y(X)

    pl.semaphore_wait(barrier, nb - 1 + ahead(1))

    order = [slice(x, x + 1) for x in (0, nx - 1, 1, nx - 2)] + ([slice(2, nx - 2)] if nx > 4 else [])
    for w in (1, 0):
        for i, x in enumerate(order):
            x = pl.ds(x.start, x.stop - x.start)
            for l in range(levels):
                remote(
                    bk.at[w, :, x], saved.at[l, w, :, x], ss.at[0], sr.at[w, i], dom, flip(l)
                ).start()

    def fetched(w, i):
        x = order[i]
        part = saved.at[:, w, :, pl.ds(x.start, x.stop - x.start)]
        pltpu.make_async_copy(part, part, sr.at[w, i]).wait()

    greet_near(know.at[0])
    for sx in (-1, 1):
        send_x(X, sx, 0)
    for sy in (-1, 1):
        send_y(X, sy)

    coef[...] = jnp.zeros(coef.shape, f32)
    red[...] = jnp.zeros(red.shape, f32)
    for x in (0, nx + 1):
        lpad[:, x] = jnp.zeros((3, ny + 2 * Y0, nz), f32)
    for y in (0, Y0 + ny):
        lpad[:, 1:nx + 1, y:y + Y0, :] = jnp.zeros((3, nx, Y0, nz), f32)
    for pad, deep in ((upad, 2), (apad, 1), (bpad, 1)):
        for y in (0, Y0 + ny):
            pad[:, deep:nx + deep, y:y + Y0, :] = jnp.zeros((3, nx, Y0, nz), f32)
    for strip in (urim, arim, brim):
        for x in (0, nx + 1):
            strip[:, :, x:x + 1, :] = jnp.zeros((2, 3, 1, nz), f32)
    invs[...] = 1.0 / stiff[...]
    inv_centre = [1.0 / jnp.full((1, nz), centre[a], f32) for a in range(3)]
    for a in range(3):
        inv[a] = 1.0 / (stiff[...] * stiff[...] * centre[a])

    pl.semaphore_wait(know.at[0], nb - 1 + ahead(1))
    if len(strides) > 1:
        greet_dom(know.at[1], strides[1])
    for q in range(4):
        pack_c(X, q, 0)
    for q in range(4):
        send_c(X, q, 0)

    def pick(value, l_of):
        got = l_of(0)
        for l in range(1, levels):
            got = jnp.where(bit_here == l, l_of(l), got)
        return jnp.where(me_failed, got, value)

    def start_field(x):
        for a in range(3):
            p0 = pick(p_in[a, x], lambda l: saved[l, 1, a, x])
            own[0, a, x] = p0
            upad[a, x.start + 2:x.stop + 2, inner, :] = p0 * stiff[x]

    loads["p"].wait()
    for i, x in enumerate(order):
        fetched(1, i)
        start_field(x)
        if i < 4:
            send_xc(U, (-1, 1)[i % 2], i // 2)
    pack_y(U)
    for sy in (-1, 1):
        send_y(U, sy)

    def start_keep(w, x):
        for l in range(levels):
            remote(own.at[w, :, x], brecv.at[l, w, :, x], bs.at[0], br.at[0], dom, flip(l)).start()

    start_keep(0, pl.ds(0, nx - 1))
    from_own(upad, 2, img.at[0])
    def know_step(i):
        pl.semaphore_wait(know.at[i], ahead(strides[i]))
        if i + 1 < len(strides):
            greet_dom(know.at[i + 1], strides[i + 1])


    def second_field(x):
        for a in range(3):
            s = stiff[x]
            restored_z = pick(0.0, lambda l: saved[l, 1, a, x]) - beta[0] * pick(0.0, lambda l: saved[l, 0, a, x])
            restored_r = restored_z * (s * s * centre[a])
            z0 = jnp.where(me_failed, restored_z, inv[a, x] * r_in[a, x])
            r0[a, x] = jnp.where(me_failed, restored_r, r_in[a, x])
            target[a, x] = rhs[a, x] - restored_r
            own[1, a, x] = z0
            apad[a, x.start + 1:x.stop + 1, inner, :] = z0 * s

    for name in ("r", "rhs"):
        loads[name].wait()
    touched = set()
    for i, x in enumerate(order):
        fetched(0, i)
        second_field(x)
        if i == 1 and len(strides) > 1:
            know_step(1)
        if i < 2:
            send_xc(A, (-1, 1)[i], 0)
        if i == len(order) - 1:
            pack_y(A)
            for sy in (-1, 1):
                send_y(A, sy)
            start_keep(0, pl.ds(nx - 1, 1))
            start_keep(1, pl.ds(0, nx))
        for source in range(x.start, x.stop):
            from_row(apad, 1, img.at[1], source, touched)

    def strip_of(h, strip):
        for i in range(2):
            for b in range(3):
                strip[i, b, 1:nx + 1, :] = h.yrecv[i, b, 0 if i else h.depth - 1]

    take(U, 0)
    strip_of(U, urim)
    from_rim(upad, 2, urim, img.at[0])
    for a in range(3):
        b0 = img[0, a] * inv_centre[a]
        bpad[a, 1:nx + 1, inner, :] = b0
        own[2, a] = b0 * invs[...]
    from_own(bpad, 1, img.at[2])

    def of_u(a):
        return upad[a, 2:nx + 2, inner, :]

    def of_z(a):
        return apad[a, 1:nx + 1, inner, :]

    def of_b(a):
        return bpad[a, 1:nx + 1, inner, :]

    def dot(left, right):
        total = None
        for a in range(3):
            t = left(a) * right(a)
            total = t if total is None else total + t
        return jnp.sum(jnp.sum(total, axis=0), axis=0, keepdims=True)

    red[0:1, :] = dot(lambda a: r0[a], lambda a: own[1, a])
    red[1:2, :] = dot(of_u, lambda a: img[0, a])
    red[2:3, :] = dot(of_z, lambda a: img[0, a])
    red[3:4, :] = dot(of_b, lambda a: img[0, a])
    unpack_y(U, (0, nx - 1))
    def edges(layers):
        for b in range(3):
            for i in range(2):
                y = Y0 + (ny - 1 if i else 0)
                for q, (sx, sy) in enumerate(CORNERS):
                    if (sy > 0) == bool(i):
                        for e in layers:
                            x = nx + 2 + e if sx > 0 else 1 - e
                            edge[i, b, 0 if i else 2, x:x + 1, :] = upad[b, x, y:y + 1, :]
                            for d in range(2):
                                edge[i, b, i + d, x:x + 1, :] = cur[q, e, b, d:d + 1, :]

    for b in range(3):
        for i in range(2):
            for d in range(2):
                edge[i, b, i + d, 2:nx + 2, :] = yur[i, b, d]
            y = Y0 + (ny - 1 if i else 0)
            for x in range(2, nx + 2):
                edge[i, b, 0 if i else 2, x:x + 1, :] = upad[b, x, y:y + 1, :]
    edges((0,))
    take(U, 1)
    edges((1,))

    rim = stencil(lambda b, dx, dy, g: upad[b, (nx + 1 if g else 0) + dx, Y0 - 1 + dy:Y0 - 1 + dy + ny, :], 2)
    for a in range(3):
        for g, sx in enumerate((-1, 1)):
            b0 = rim[a][g] * inv_centre[a]
            bpad[a, nx + 1 if g else 0, inner, :] = jnp.where(has(sx, 0), b0, 0.0)
    rim = stencil(lambda b, dx, dy, g: edge[g, b, dy, dx:dx + nx + 2, :], 2)
    row = lax.broadcasted_iota(jnp.int32, (nx + 2, nz), 0)
    first_in = jnp.where(dom > 0, 0, 1)
    last_in = jnp.where(dom < nd - 1, nx + 1, nx)
    inside = jnp.logical_and(row >= first_in, row <= last_in)
    for a in range(3):
        for g, sy in enumerate((-1, 1)):
            b0 = jnp.where(inside, rim[a][g] * inv_centre[a], 0.0)
            b0 = jnp.where(has(0, sy), b0, 0.0)
            ytmp[g, a] = b0
            brim[g, a, 1:nx + 1, :] = b0[1:nx + 1]
    for a in range(3):
        for g in range(2):
            y = Y0 + ny if g else Y0 - 1
            for x in (0, nx + 1):
                bpad[a, x, y:y + 1, :] = ytmp[g, a, x:x + 1, :]
    from_rim(bpad, 1, brim, img.at[2])

    red[5:6, :] = dot(of_z, lambda a: img[2, a])
    red[6:7, :] = dot(of_b, lambda a: img[2, a])
    take(A, 0)
    strip_of(A, arim)
    from_rim(apad, 1, arim, img.at[1])
    red[4:5, :] = dot(of_z, lambda a: img[1, a])

    rows = lax.broadcasted_iota(jnp.int32, (8, nz), 0)
    diagonal = rows == lax.broadcasted_iota(jnp.int32, (8, nz), 1)
    each = jnp.sum(red[...], axis=1, keepdims=True)
    red1[...] = jnp.sum(jnp.where(diagonal, each, 0.0), axis=0, keepdims=True)
    for i in range(2, len(strides)):
        know_step(i)
    n = nd * nb
    me = dom * nb + bud
    rall[me] = red1[...]
    bits = [(1 << i) * (1 - 2 * lax.rem(dom // (1 << i), 2)) for i in range((nd - 1).bit_length())]
    for mask in range(nd - 1, -1, -1):
        to = dom + sum(bit for i, bit in enumerate(bits) if mask >> i & 1)
        for j in range(nb):
            if mask or j:
                remote(red1, rall.at[me], ds.at[0], dr.at[0], to, lax.rem(bud + j, nb)).start()

    def every():
        part = rall.at[pl.ds(0, n - 1)]
        return remote(part, part, ds.at[0], dr.at[0], dom, bud)

    start_keep(2, pl.ds(0, nx))

    take(X, 0)
    unpack_y(X, range(nx))
    apply(xpad, 1, img3)
    centre_value = (HIGH + LOW) / 2.0
    half_width = (HIGH - LOW) / 2.0
    ratio_value = centre_value / half_width
    weight = 1.0 / ratio_value
    for a in range(3):
        t = target[a] - img3[a] * stiff[...]
        d = inv[a] * t / centre_value
        target[a] = t
        update[a] = d
        solved[a] = d
        lpad[a, 1:nx + 1, inner, :] = d * stiff[...]
    for sweep in range(SWEEPS - 1):
        apply(lpad, 1, img3)
        weight_next = 1.0 / (2.0 * ratio_value - weight)
        for a in range(3):
            remain = target[a] - img3[a] * stiff[...]
            d = weight_next * weight * update[a] + (2.0 * weight_next / half_width) * (inv[a] * remain)
            y = solved[a] + d
            update[a] = d
            solved[a] = y
            if sweep < SWEEPS - 2:
                lpad[a, 1:nx + 1, inner, :] = y * stiff[...]
        weight = weight_next

    for a in range(3):
        x_out[a] = jnp.where(me_failed, solved[a], x_in[a])
    s_out[...] = stiff[...]
    end_halos()

    def all_of(ref, sem):
        return remote(ref, ref, sem.at[0], sem.at[0], dom, bud)

    all_of(saved, ss).wait_send()
    all_of(brecv, bs).wait_send()
    every().wait_send()
    pltpu.make_async_copy(brecv, brecv, br.at[0]).wait()
    for w in range(3):
        for a in range(3):
            got = brecv[0, w, a]
            for l in range(1, levels):
                got = jnp.where(bit_here == l, brecv[l, w, a], got)
            other[w, a] = got

    every().wait_recv()
    total = jnp.sum(rall[...], axis=0)
    sums = jnp.sum(jnp.where(diagonal, jnp.broadcast_to(total, (8, nz)), 0.0), axis=1, keepdims=True)
    g0, c0, e0, f0, h0, h1, h2 = [jnp.broadcast_to(sums[j:j + 1], (1, nz)) for j in range(7)]
    alpha0 = g0 / c0
    g1 = g0 - 2.0 * alpha0 * e0 + alpha0 * alpha0 * f0
    beta0 = g1 / g0
    c1 = (
        h0 - 2.0 * alpha0 * h1 + alpha0 * alpha0 * h2
        + 2.0 * beta0 * (e0 - alpha0 * f0) + beta0 * beta0 * c0
    )
    alpha1 = g1 / c1
    coef[0:1, :] = alpha0
    coef[1:2, :] = beta0
    coef[2:3, :] = alpha1


def finish(x0, r0, own, other, img, stiff, coef, x_out, r_out, b_out, xs, rs, bs, sems):
    copies = [pltpu.make_async_copy(other.at[0], b_out.at[0], sems.at[9])]
    copies[0].start()
    alpha0, beta0, alpha1 = coef[0:1, :], coef[1:2, :], coef[2:3, :]
    alpha0, beta0, alpha1 = alpha0[None], beta0[None], alpha1[None]
    for a in range(3):
        bs[a] = other[1, a] - alpha0 * other[2, a] + beta0 * other[0, a]
        p0 = own[0, a]
        p1 = own[1, a] - alpha0 * own[2, a] + beta0 * p0
        xs[a] = x0[a] + alpha0 * p0 + alpha1 * p1
        t0 = img[0, a]
        q1 = img[1, a] - alpha0 * img[2, a] + beta0 * t0
        rs[a] = r0[a] - stiff[...] * (alpha0 * t0 + alpha1 * q1)
        for i, (src, dst) in enumerate((
            (bs.at[a], b_out.at[1, a]), (xs.at[a], x_out.at[a]), (rs.at[a], r_out.at[a]),
        )):
            copies.append(pltpu.make_async_copy(src, dst, sems.at[a * 3 + i]))
            copies[-1].start()
    for c in copies:
        c.wait()


def on_device(nd, nb, rhs, stiff, coupling, x_in, r_in, p_in, backup_in, beta, fc, bb):
    levels = nb.bit_length() - 1
    nx, ny, nz = stiff.shape
    f32 = jnp.float32
    vmem = pl.BlockSpec(memory_space=pltpu.VMEM)
    smem = pl.BlockSpec(memory_space=pltpu.SMEM)
    hbm = pl.BlockSpec(memory_space=pltpu.HBM)
    field = (3, nx, ny, nz)
    dma = pltpu.SemaphoreType.DMA

    def v(*shape):
        return pltpu.VMEM(shape, f32)

    def rim(deep):
        return v(3, nx + 2 * deep, ny + 2 * Y0, nz)

    def strips(deep):
        return [v(2, 3, deep, nx, nz)] * 2 + [v(4, deep, 3, deep, nz)] * 2

    parts = pl.pallas_call(
        functools.partial(kernel, nd, nb, levels),
        out_shape=(
            v(*field), v(*field), v(3, *field), v(3, *field), v(3, *field), v(nx, ny, nz), v(8, nz),
        ),
        in_specs=[hbm] * 7 + [smem] * 3,
        out_specs=(vmem,) * 7,
        scratch_shapes=[
            v(*field), v(nx, ny, nz), pltpu.SMEM((3, 3, 27), f32), v(*field), v(*field), v(*field), v(2, *field),
            dma((7,)),
            rim(2), rim(1), rim(1), rim(1), rim(1),
            *strips(2), *strips(1), *strips(1),
            v(2, 3, 3, nx + 4, nz), *[v(2, 3, nx + 2, nz)] * 3, v(2, 3, nx + 2, nz), v(levels, 2, *field), v(levels, 3, *field),
            v(*field), v(nx, ny, nz), v(*field), v(*field), v(*field), v(*field),
            v(8, nz), v(1, nz), v(nd * nb, 1, nz),
            v(3, ny, nz), v(3, 2, nx, nz), v(3, 1, nx, nz), v(3, 2, nz), v(3, 1, nz),
            v(max(12 * ny, halo_rows(nx, ny, 2)), 1, nz),
            dma((8,)), dma((2,)), dma((1,)), dma((1,)),
            dma((1,)), dma((2, 4 if nx == 4 else 5)),
            dma((1,)), dma((1,)), dma((1,)), dma((1,)),
            pltpu.SemaphoreType.REGULAR((max((nd - 1).bit_length(), 1),)),
        ],
        compiler_params=pltpu.CompilerParams(
            collective_id=0, has_side_effects=True, vmem_limit_bytes=40 * 1024 * 1024
        ),
    )(*[pltpu.with_memory_space_constraint(v, pltpu.HBM) for v in (
        rhs, stiff, jnp.transpose(coupling, (1, 2, 0)), x_in, r_in, p_in, backup_in
    )], beta, fc, bb)
    return pl.pallas_call(
        finish,
        out_shape=(
            pltpu.HBM(field, f32), pltpu.HBM(field, f32), pltpu.HBM((2,) + field, f32),
        ),
        in_specs=[vmem] * 7,
        out_specs=(hbm, hbm, hbm),
        scratch_shapes=[
            pltpu.VMEM(field, f32), pltpu.VMEM(field, f32), pltpu.VMEM(field, f32), dma((10,)),
        ],
        compiler_params=pltpu.CompilerParams(vmem_limit_bytes=8 * 1024 * 1024),
    )(*parts)


def solution(mesh):
    nd, nb = mesh.shape["dom"], mesh.shape["bud"]
    placed = (
        P(None, "dom", "bud", None),
        P("dom", "bud", None),
        P(),
        P(None, "dom", "bud", None),
        P(None, "dom", "bud", None),
        P(None, "dom", "bud", None),
        P(None, None, "dom", "bud", None),
        P(),
        P("dom"),
        P("dom"),
    )
    return jax.shard_map(
        functools.partial(on_device, nd, nb),
        mesh=mesh,
        in_specs=placed,
        out_specs=(
            P(None, "dom", "bud", None),
            P(None, "dom", "bud", None),
            P(None, None, "dom", "bud", None),
        ),
        check_vma=False,
    )
```

```python
import functools

import jax
import jax.numpy as jnp
from jax import lax
from jax.experimental import pallas as pl
from jax.experimental.pallas import tpu as pltpu
from jax.sharding import PartitionSpec as P

SWEEPS = 4
LOW = 0.01
HIGH = 1.99
Y0 = 8
CORNERS = [(sx, sy) for sx in (-1, 1) for sy in (-1, 1)]


class Halo:
    def __init__(self, depth, pad, ysend, yrecv, csend, crecv, recv, zero):
        self.depth, self.pad = depth, pad
        self.ysend, self.yrecv, self.csend, self.crecv = ysend, yrecv, csend, crecv
        self.recv, self.zero = recv, zero


def halo_rows(nx, ny, depth):
    return 6 * ny + 6 * depth * nx + 12 * depth


def kernel(
    nd, nb, levels,
    rhs_h, stiff_h, cpl_h, x_h, r_h, p_h, bk_h, beta, fc, bb,
    x_out, r0, own, other, img, s_out, coef,
    rhs, stiff, cpl, x_in, r_in, p_in, bk, in_sems,
    upad, apad, xpad, bpad, lpad,
    yus, yur, cus, cur, yas, yar, cas, car, yxs, yxr, cxs, cxr,
    edge, urim, arim, brim, ytmp, saved, brecv,
    inv, invs, img3, target, solved, update,
    red, red1, rall,
    zx, zy2, zy1, zc2, zc1, dummy,
    hs, ur, ar, xr, ss, sr, bs, br, ds, dr, know,
):
    nx, ny, nz = stiff.shape
    step = 2 if nx % 2 == 0 else 1
    dom, bud = lax.axis_index("dom"), lax.axis_index("bud")
    f32 = jnp.float32

    def has(sx, sy):
        ok = None
        for cond in (
            ([dom > 0] if sx < 0 else [dom < nd - 1] if sx > 0 else [])
            + ([bud > 0] if sy < 0 else [bud < nb - 1] if sy > 0 else [])
        ):
            ok = cond if ok is None else jnp.logical_and(ok, cond)
        return ok

    def remote(src, dst, send, recv, d, b):
        return pltpu.make_async_remote_copy(
            src_ref=src, dst_ref=dst, send_sem=send, recv_sem=recv,
            device_id={"dom": d, "bud": b}, device_id_type=pl.DeviceIdType.MESH,
        )

    def flip(level):
        stride = 1 << level
        return bud + stride * (1 - 2 * (lax.rem(bud // stride, 2)))

    barrier = pltpu.get_barrier_semaphore()

    def greet(sem, d, b):
        pl.semaphore_signal(
            sem, inc=1, device_id={"dom": d, "bud": b},
            device_id_type=pl.DeviceIdType.MESH,
        )

    def ahead(stride):
        return jnp.where(dom >= stride, 1, 0) + jnp.where(dom < nd - stride, 1, 0)

    def greet_dom(sem, stride):
        @pl.when(dom >= stride)
        def _():
            greet(sem, dom - stride, bud)

        @pl.when(dom < nd - stride)
        def _():
            greet(sem, dom + stride, bud)

    def greet_near(sem):
        for j in range(1, nb):
            greet(sem, dom, lax.rem(bud + j, nb))
        greet_dom(sem, 1)

    strides = [1 << i for i in range(max(nd - 1, 1).bit_length())]
    greet_near(barrier)

    loads = {}
    for i, (name, src, dst) in enumerate((
        ("bk", bk_h, bk), ("cpl", cpl_h, cpl), ("stiff", stiff_h, stiff), ("x", x_h, x_in),
        ("p", p_h, p_in), ("r", r_h, r_in), ("rhs", rhs_h, rhs),
    )):
        loads[name] = pltpu.make_async_copy(src, dst, in_sems.at[i])
        loads[name].start()

    for zero in (zx, zy2, zy1, zc2, zc1):
        zero[...] = jnp.zeros(zero.shape, f32)
    U = Halo(2, upad, yus, yur, cus, cur, ur, (zx, zy2, zc2))
    A = Halo(1, apad, yas, yar, cas, car, ar, (zx, zy1, zc1))
    X = Halo(1, xpad, yxs, yxr, cxs, cxr, xr, (zx, zy1, zc1))
    inner = pl.ds(Y0, ny)

    def either(sx, sy, there, beyond):
        @pl.when(has(sx, sy))
        def _():
            there().start()

        @pl.when(jnp.logical_not(has(sx, sy)))
        def _():
            beyond().start()

    def send_x(h, sx, d):
        deep = h.depth
        low, high = deep - 1 - d, deep + nx + d
        src = deep + (nx - 1 - d if sx > 0 else d)
        to, own_side = (low, high) if sx > 0 else (high, low)
        either(sx, 0, lambda: remote(
            h.pad.at[:, src, inner, :], h.pad.at[:, to, inner, :], hs.at[1 if sx > 0 else 0], h.recv.at[d],
            dom + sx, bud,
        ), lambda: pltpu.make_async_copy(h.zero[0], h.pad.at[:, own_side, inner, :], h.recv.at[d]))

    def send_y(h, sy):
        i = 1 if sy > 0 else 0
        either(0, sy, lambda: remote(
            h.ysend.at[i], h.yrecv.at[1 - i], hs.at[2 + i], h.recv.at[0], dom, bud + sy,
        ), lambda: pltpu.make_async_copy(h.zero[1], h.yrecv.at[i], h.recv.at[0]))

    def send_c(h, q, e):
        sx, sy = CORNERS[q]
        either(sx, sy, lambda: remote(
            h.csend.at[q, e], h.crecv.at[3 - q, e], hs.at[4 + q], h.recv.at[e], dom + sx, bud + sy,
        ), lambda: pltpu.make_async_copy(h.zero[2], h.crecv.at[q, e], h.recv.at[e]))

    def send_xc(h, sx, d):
        for q in range(4):
            if CORNERS[q][0] == sx:
                pack_c(h, q, d)
        for q in range(4):
            if CORNERS[q][0] == sx:
                send_c(h, q, d)
        send_x(h, sx, d)

    def end_halos():
        deeps = (2, 1, 1)
        for i, (sx, sy, rows) in enumerate(
            [(sx, 0, 3 * ny * sum(deeps)) for sx in (-1, 1)]
            + [(0, sy, 3 * nx * sum(deeps)) for sy in (-1, 1)]
            + [(sx, sy, 3 * sum(d * d for d in deeps)) for sx, sy in CORNERS]
        ):
            @pl.when(has(sx, sy))
            def _(i=i, sx=sx, sy=sy, rows=rows):
                part = dummy.at[pl.ds(0, rows)]
                remote(part, part, hs.at[i], hs.at[i], dom + sx, bud + sy).wait_send()

    def pack_y(h):
        deep = h.depth
        for i in range(2):
            for b in range(3):
                for d in range(deep):
                    y = Y0 + (ny - deep + d if i else d)
                    for x in range(nx):
                        h.ysend[i, b, d, x:x + 1, :] = h.pad[b, deep + x, y:y + 1, :]

    def pack_c(h, q, e):
        deep = h.depth
        sx, sy = CORNERS[q]
        x = deep + (nx - 1 - e if sx > 0 else e)
        for b in range(3):
            for d in range(deep):
                y = Y0 + (ny - deep + d if sy > 0 else d)
                h.csend[q, e, b, d:d + 1, :] = h.pad[b, x, y:y + 1, :]

    def unpack_y(h, xs):
        deep = h.depth
        for i in range(2):
            y, d = (Y0 + ny, 0) if i else (Y0 - 1, deep - 1)
            for b in range(3):
                for x in xs:
                    h.pad[b, deep + x, y:y + 1, :] = h.yrecv[i, b, d, x:x + 1, :]

    def unpack_c(h, e):
        deep = h.depth
        for q, (sx, sy) in enumerate(CORNERS):
            x = deep + nx + e if sx > 0 else deep - 1 - e
            y, d = (Y0 + ny, 0) if sy > 0 else (Y0 - 1, deep - 1)
            for b in range(3):
                h.pad[b, x, y:y + 1, :] = h.crecv[q, e, b, d:d + 1, :]

    def take(h, d):
        rows = 6 * ny + 12 * h.depth + (6 * h.depth * nx if d == 0 else 0)
        part = dummy.at[pl.ds(0, rows)]
        pltpu.make_async_copy(part, part, h.recv.at[d]).wait()
        unpack_c(h, d)

    def stencil(load, groups):
        acc = [[[None] * groups for _ in range(3)] for _ in range(3)]
        for dx in range(3):
            for dy in range(3):
                for b in range(3):
                    ws = [load(b, dx, dy, g) for g in range(groups)]
                    if all(w is None for w in ws):
                        continue
                    for dz in range(3):
                        o = (dx * 3 + dy) * 3 + dz
                        for a in range(3):
                            for g in range(groups):
                                if ws[g] is None:
                                    continue
                                term = cpl[a, b, o] * ws[g]
                                old = acc[dz][a][g]
                                acc[dz][a][g] = term if old is None else old + term
        lane = lax.broadcasted_iota(jnp.int32, acc[0][0][0].shape, 1)

        def joined(a, g):
            before = jnp.where(lane == 0, 0.0, pltpu.roll(acc[0][a][g], 1, 1))
            after = jnp.where(lane == nz - 1, 0.0, pltpu.roll(acc[2][a][g], nz - 1, 1))
            return acc[1][a][g] + before + after

        return [[joined(a, g) for g in range(groups)] for a in range(3)]

    def apply(pad, deep, out):
        @pl.loop(0, nx // step)
        def _(j):
            x = j * step
            got = stencil(
                lambda b, dx, dy, g: pad[b, x + (g + deep - 1 + dx), Y0 - 1 + dy:Y0 - 1 + dy + ny, :], step
            )
            for a in range(3):
                for g in range(step):
                    out[a, x + g] = got[a][g]

    def from_own(pad, deep, out):
        for x in range(0, nx, step):
            got = stencil(
                lambda b, dx, dy, g: pad[b, x + g + deep - 1 + dx, Y0 - 1 + dy:Y0 - 1 + dy + ny, :]
                if 0 <= x + g + dx - 1 < nx else None, step
            )
            for a in range(3):
                for g in range(step):
                    out[a, x + g] = got[a][g]

    def from_row(pad, deep, out, source, touched):
        targets = [x for x in (source - 1, source, source + 1) if 0 <= x < nx]
        for xs in (targets[:2], targets[2:]):
            if not xs:
                continue
            got = stencil(
                lambda b, dx, dy, g: pad[b, source + deep, Y0 - 1 + dy:Y0 - 1 + dy + ny, :]
                if dx == source - xs[g] + 1 else None, len(xs)
            )
            for a in range(3):
                for g, x in enumerate(xs):
                    out[a, x] = out[a, x] + got[a][g] if x in touched else got[a][g]
            touched.update(xs)

    def from_rim(pad, deep, strip, out):
        got = stencil(
            lambda b, dx, dy, g: strip[g, b, dx:dx + nx, :] if dy == 2 * g else None, 2
        )
        for a in range(3):
            for g in range(2):
                ytmp[g, a, 0:nx, :] = got[a][g]
        got = stencil(
            lambda b, dx, dy, g: pad[b, deep + nx if g else deep - 1, Y0 - 1 + dy:Y0 - 1 + dy + ny, :]
            if dx == 2 * g else None, 2
        )
        for a in range(3):
            for g, x in enumerate((0, nx - 1)):
                out[a, x] = out[a, x] + got[a][g]
        for a in range(3):
            for g, y in enumerate((0, ny - 1)):
                for x in range(nx):
                    out[a, x, y:y + 1, :] = out[a, x, y:y + 1, :] + ytmp[g, a, x:x + 1, :]

    loads["bk"].wait()
    pl.semaphore_wait(barrier, nb - 1 + ahead(1))

    order = [slice(x, x + 1) for x in (0, nx - 1, 1, nx - 2)] + ([slice(2, nx - 2)] if nx > 4 else [])
    for w in (1, 0):
        for i, x in enumerate(order):
            x = pl.ds(x.start, x.stop - x.start)
            for l in range(levels):
                remote(
                    bk.at[w, :, x], saved.at[l, w, :, x], ss.at[0], sr.at[w, i], dom, flip(l)
                ).start()

    def fetched(w, i):
        x = order[i]
        part = saved.at[:, w, :, pl.ds(x.start, x.stop - x.start)]
        pltpu.make_async_copy(part, part, sr.at[w, i]).wait()

    greet_near(know.at[0])
    for name in ("cpl", "stiff", "x"):
        loads[name].wait()
    me_failed = jnp.full((1, ny, nz), fc[0], jnp.int32) == bud
    bit_here = jnp.full((1, ny, nz), bb[0], jnp.int32)
    centre = [cpl[a, a, 13] for a in range(3)]
    for a in range(3):
        xpad[a, 1:nx + 1, inner, :] = jnp.where(me_failed, 0.0, x_in[a] * stiff[...])
    pack_y(X)

    for sx in (-1, 1):
        send_x(X, sx, 0)
    for sy in (-1, 1):
        send_y(X, sy)

    coef[...] = jnp.zeros(coef.shape, f32)
    red[...] = jnp.zeros(red.shape, f32)
    for x in (0, nx + 1):
        lpad[:, x] = jnp.zeros((3, ny + 2 * Y0, nz), f32)
    for y in (0, Y0 + ny):
        lpad[:, 1:nx + 1, y:y + Y0, :] = jnp.zeros((3, nx, Y0, nz), f32)
    for pad, deep in ((upad, 2), (apad, 1), (bpad, 1)):
        for y in (0, Y0 + ny):
            pad[:, deep:nx + deep, y:y + Y0, :] = jnp.zeros((3, nx, Y0, nz), f32)
    for strip in (urim, arim, brim):
        for x in (0, nx + 1):
            strip[:, :, x:x + 1, :] = jnp.zeros((2, 3, 1, nz), f32)
    invs[...] = 1.0 / stiff[...]
    inv_centre = [1.0 / jnp.full((1, nz), centre[a], f32) for a in range(3)]
    for a in range(3):
        inv[a] = 1.0 / (stiff[...] * stiff[...] * centre[a])

    pl.semaphore_wait(know.at[0], nb - 1 + ahead(1))
    if len(strides) > 1:
        greet_dom(know.at[1], strides[1])
    for q in range(4):
        pack_c(X, q, 0)
    for q in range(4):
        send_c(X, q, 0)

    def pick(value, l_of):
        got = l_of(0)
        for l in range(1, levels):
            got = jnp.where(bit_here == l, l_of(l), got)
        return jnp.where(me_failed, got, value)

    def start_field(x):
        for a in range(3):
            p0 = pick(p_in[a, x], lambda l: saved[l, 1, a, x])
            own[0, a, x] = p0
            upad[a, x.start + 2:x.stop + 2, inner, :] = p0 * stiff[x]

    loads["p"].wait()
    for i, x in enumerate(order):
        fetched(1, i)
        start_field(x)
        if i < 4:
            send_xc(U, (-1, 1)[i % 2], i // 2)
    pack_y(U)
    for sy in (-1, 1):
        send_y(U, sy)

    def start_keep(w, x):
        for l in range(levels):
            remote(own.at[w, :, x], brecv.at[l, w, :, x], bs.at[0], br.at[0], dom, flip(l)).start()

    start_keep(0, pl.ds(0, nx - 1))
    from_own(upad, 2, img.at[0])
    def know_step(i):
        pl.semaphore_wait(know.at[i], ahead(strides[i]))
        if i + 1 < len(strides):
            greet_dom(know.at[i + 1], strides[i + 1])


    def second_field(x):
        for a in range(3):
            s = stiff[x]
            restored_z = pick(0.0, lambda l: saved[l, 1, a, x]) - beta[0] * pick(0.0, lambda l: saved[l, 0, a, x])
            restored_r = restored_z * (s * s * centre[a])
            z0 = jnp.where(me_failed, restored_z, inv[a, x] * r_in[a, x])
            r0[a, x] = jnp.where(me_failed, restored_r, r_in[a, x])
            target[a, x] = rhs[a, x] - restored_r
            own[1, a, x] = z0
            apad[a, x.start + 1:x.stop + 1, inner, :] = z0 * s

    for name in ("r", "rhs"):
        loads[name].wait()
    touched = set()
    for i, x in enumerate(order):
        fetched(0, i)
        second_field(x)
        if i == 1 and len(strides) > 1:
            know_step(1)
        if i < 2:
            send_xc(A, (-1, 1)[i], 0)
        if i == len(order) - 1:
            pack_y(A)
            for sy in (-1, 1):
                send_y(A, sy)
            start_keep(0, pl.ds(nx - 1, 1))
            start_keep(1, pl.ds(0, nx - 1))
        for source in range(x.start, x.stop):
            from_row(apad, 1, img.at[1], source, touched)

    def strip_of(h, strip):
        for i in range(2):
            for b in range(3):
                strip[i, b, 1:nx + 1, :] = h.yrecv[i, b, 0 if i else h.depth - 1]

    take(U, 0)
    strip_of(U, urim)
    from_rim(upad, 2, urim, img.at[0])
    for a in range(3):
        b0 = img[0, a] * inv_centre[a]
        bpad[a, 1:nx + 1, inner, :] = b0
    from_own(bpad, 1, img.at[2])

    def of_u(a):
        return upad[a, 2:nx + 2, inner, :]

    def of_z(a):
        return apad[a, 1:nx + 1, inner, :]

    def of_b(a):
        return bpad[a, 1:nx + 1, inner, :]

    def dot(left, right):
        total = None
        for a in range(3):
            t = left(a) * right(a)
            total = t if total is None else total + t
        return jnp.sum(jnp.sum(total, axis=0), axis=0, keepdims=True)

    red[0:1, :] = dot(lambda a: r0[a], lambda a: own[1, a])
    red[1:2, :] = dot(of_u, lambda a: img[0, a])
    red[2:3, :] = dot(of_z, lambda a: img[0, a])
    red[3:4, :] = dot(of_b, lambda a: img[0, a])
    unpack_y(U, (0, nx - 1))
    def edges(layers):
        for b in range(3):
            for i in range(2):
                y = Y0 + (ny - 1 if i else 0)
                for q, (sx, sy) in enumerate(CORNERS):
                    if (sy > 0) == bool(i):
                        for e in layers:
                            x = nx + 2 + e if sx > 0 else 1 - e
                            edge[i, b, 0 if i else 2, x:x + 1, :] = upad[b, x, y:y + 1, :]
                            for d in range(2):
                                edge[i, b, i + d, x:x + 1, :] = cur[q, e, b, d:d + 1, :]

    for b in range(3):
        for i in range(2):
            for d in range(2):
                edge[i, b, i + d, 2:nx + 2, :] = yur[i, b, d]
            y = Y0 + (ny - 1 if i else 0)
            for x in range(2, nx + 2):
                edge[i, b, 0 if i else 2, x:x + 1, :] = upad[b, x, y:y + 1, :]
    edges((0,))
    take(U, 1)
    edges((1,))

    rim = stencil(lambda b, dx, dy, g: upad[b, (nx + 1 if g else 0) + dx, Y0 - 1 + dy:Y0 - 1 + dy + ny, :], 2)
    for a in range(3):
        for g, sx in enumerate((-1, 1)):
            b0 = rim[a][g] * inv_centre[a]
            bpad[a, nx + 1 if g else 0, inner, :] = jnp.where(has(sx, 0), b0, 0.0)
    rim = stencil(lambda b, dx, dy, g: edge[g, b, dy, dx:dx + nx + 2, :], 2)
    row = lax.broadcasted_iota(jnp.int32, (nx + 2, nz), 0)
    first_in = jnp.where(dom > 0, 0, 1)
    last_in = jnp.where(dom < nd - 1, nx + 1, nx)
    inside = jnp.logical_and(row >= first_in, row <= last_in)
    for a in range(3):
        for g, sy in enumerate((-1, 1)):
            b0 = jnp.where(inside, rim[a][g] * inv_centre[a], 0.0)
            b0 = jnp.where(has(0, sy), b0, 0.0)
            ytmp[g, a] = b0
            brim[g, a, 1:nx + 1, :] = b0[1:nx + 1]
    for a in range(3):
        for g in range(2):
            y = Y0 + ny if g else Y0 - 1
            for x in (0, nx + 1):
                bpad[a, x, y:y + 1, :] = ytmp[g, a, x:x + 1, :]
    from_rim(bpad, 1, brim, img.at[2])

    red[5:6, :] = dot(of_z, lambda a: img[2, a])
    red[6:7, :] = dot(of_b, lambda a: img[2, a])
    take(A, 0)
    strip_of(A, arim)
    from_rim(apad, 1, arim, img.at[1])
    red[4:5, :] = dot(of_z, lambda a: img[1, a])

    rows = lax.broadcasted_iota(jnp.int32, (8, nz), 0)
    diagonal = rows == lax.broadcasted_iota(jnp.int32, (8, nz), 1)
    each = jnp.sum(red[...], axis=1, keepdims=True)
    red1[...] = jnp.sum(jnp.where(diagonal, each, 0.0), axis=0, keepdims=True)
    for i in range(2, len(strides)):
        know_step(i)
    n = nd * nb
    me = dom * nb + bud
    rall[me] = red1[...]
    bits = [(1 << i) * (1 - 2 * lax.rem(dom // (1 << i), 2)) for i in range((nd - 1).bit_length())]
    for mask in range(nd - 1, -1, -1):
        to = dom + sum(bit for i, bit in enumerate(bits) if mask >> i & 1)
        for j in range(nb):
            if mask or j:
                remote(red1, rall.at[me], ds.at[0], dr.at[0], to, lax.rem(bud + j, nb)).start()

    def every():
        part = rall.at[pl.ds(0, n - 1)]
        return remote(part, part, ds.at[0], dr.at[0], dom, bud)

    start_keep(1, pl.ds(nx - 1, 1))
    for a in range(3):
        own[2, a] = of_b(a) * invs[...]
    start_keep(2, pl.ds(0, nx))

    take(X, 0)
    unpack_y(X, range(nx))
    apply(xpad, 1, img3)
    centre_value = (HIGH + LOW) / 2.0
    half_width = (HIGH - LOW) / 2.0
    ratio_value = centre_value / half_width
    weight = 1.0 / ratio_value
    for a in range(3):
        t = target[a] - img3[a] * stiff[...]
        d = inv[a] * t / centre_value
        target[a] = t
        update[a] = d
        solved[a] = d
        lpad[a, 1:nx + 1, inner, :] = d * stiff[...]
    for sweep in range(SWEEPS - 1):
        apply(lpad, 1, img3)
        weight_next = 1.0 / (2.0 * ratio_value - weight)
        for a in range(3):
            remain = target[a] - img3[a] * stiff[...]
            d = weight_next * weight * update[a] + (2.0 * weight_next / half_width) * (inv[a] * remain)
            y = solved[a] + d
            update[a] = d
            solved[a] = y
            if sweep < SWEEPS - 2:
                lpad[a, 1:nx + 1, inner, :] = y * stiff[...]
        weight = weight_next

    for a in range(3):
        x_out[a] = jnp.where(me_failed, solved[a], x_in[a])
    s_out[...] = stiff[...]
    end_halos()

    def all_of(ref, sem):
        return remote(ref, ref, sem.at[0], sem.at[0], dom, bud)

    all_of(saved, ss).wait_send()
    all_of(brecv, bs).wait_send()
    every().wait_send()
    pltpu.make_async_copy(brecv, brecv, br.at[0]).wait()
    for w in range(3):
        for a in range(3):
            got = brecv[0, w, a]
            for l in range(1, levels):
                got = jnp.where(bit_here == l, brecv[l, w, a], got)
            other[w, a] = got

    every().wait_recv()
    total = jnp.sum(rall[...], axis=0)
    sums = jnp.sum(jnp.where(diagonal, jnp.broadcast_to(total, (8, nz)), 0.0), axis=1, keepdims=True)
    g0, c0, e0, f0, h0, h1, h2 = [jnp.broadcast_to(sums[j:j + 1], (1, nz)) for j in range(7)]
    alpha0 = g0 / c0
    g1 = g0 - 2.0 * alpha0 * e0 + alpha0 * alpha0 * f0
    beta0 = g1 / g0
    c1 = (
        h0 - 2.0 * alpha0 * h1 + alpha0 * alpha0 * h2
        + 2.0 * beta0 * (e0 - alpha0 * f0) + beta0 * beta0 * c0
    )
    alpha1 = g1 / c1
    coef[0:1, :] = alpha0
    coef[1:2, :] = beta0
    coef[2:3, :] = alpha1


def finish(x0, r0, own, other, img, stiff, coef, x_out, r_out, b_out, xs, rs, bs, sems):
    copies = [pltpu.make_async_copy(other.at[0], b_out.at[0], sems.at[9])]
    copies[0].start()
    alpha0, beta0, alpha1 = coef[0:1, :], coef[1:2, :], coef[2:3, :]
    alpha0, beta0, alpha1 = alpha0[None], beta0[None], alpha1[None]
    for a in range(3):
        bs[a] = other[1, a] - alpha0 * other[2, a] + beta0 * other[0, a]
        p0 = own[0, a]
        p1 = own[1, a] - alpha0 * own[2, a] + beta0 * p0
        xs[a] = x0[a] + alpha0 * p0 + alpha1 * p1
        t0 = img[0, a]
        q1 = img[1, a] - alpha0 * img[2, a] + beta0 * t0
        rs[a] = r0[a] - stiff[...] * (alpha0 * t0 + alpha1 * q1)
        for i, (src, dst) in enumerate((
            (bs.at[a], b_out.at[1, a]), (xs.at[a], x_out.at[a]), (rs.at[a], r_out.at[a]),
        )):
            copies.append(pltpu.make_async_copy(src, dst, sems.at[a * 3 + i]))
            copies[-1].start()
    for c in copies:
        c.wait()


def on_device(nd, nb, rhs, stiff, coupling, x_in, r_in, p_in, backup_in, beta, fc, bb):
    levels = nb.bit_length() - 1
    nx, ny, nz = stiff.shape
    f32 = jnp.float32
    vmem = pl.BlockSpec(memory_space=pltpu.VMEM)
    smem = pl.BlockSpec(memory_space=pltpu.SMEM)
    hbm = pl.BlockSpec(memory_space=pltpu.HBM)
    field = (3, nx, ny, nz)
    dma = pltpu.SemaphoreType.DMA

    def v(*shape):
        return pltpu.VMEM(shape, f32)

    def rim(deep):
        return v(3, nx + 2 * deep, ny + 2 * Y0, nz)

    def strips(deep):
        return [v(2, 3, deep, nx, nz)] * 2 + [v(4, deep, 3, deep, nz)] * 2

    parts = pl.pallas_call(
        functools.partial(kernel, nd, nb, levels),
        out_shape=(
            v(*field), v(*field), v(3, *field), v(3, *field), v(3, *field), v(nx, ny, nz), v(8, nz),
        ),
        in_specs=[hbm] * 7 + [smem] * 3,
        out_specs=(vmem,) * 7,
        scratch_shapes=[
            v(*field), v(nx, ny, nz), pltpu.SMEM((3, 3, 27), f32), v(*field), v(*field), v(*field), v(2, *field),
            dma((7,)),
            rim(2), rim(1), rim(1), rim(1), rim(1),
            *strips(2), *strips(1), *strips(1),
            v(2, 3, 3, nx + 4, nz), *[v(2, 3, nx + 2, nz)] * 3, v(2, 3, nx + 2, nz), v(levels, 2, *field), v(levels, 3, *field),
            v(*field), v(nx, ny, nz), v(*field), v(*field), v(*field), v(*field),
            v(8, nz), v(1, nz), v(nd * nb, 1, nz),
            v(3, ny, nz), v(3, 2, nx, nz), v(3, 1, nx, nz), v(3, 2, nz), v(3, 1, nz),
            v(max(12 * ny, halo_rows(nx, ny, 2)), 1, nz),
            dma((8,)), dma((2,)), dma((1,)), dma((1,)),
            dma((1,)), dma((2, 4 if nx == 4 else 5)),
            dma((1,)), dma((1,)), dma((1,)), dma((1,)),
            pltpu.SemaphoreType.REGULAR((max((nd - 1).bit_length(), 1),)),
        ],
        compiler_params=pltpu.CompilerParams(
            collective_id=0, has_side_effects=True, vmem_limit_bytes=40 * 1024 * 1024
        ),
    )(*[pltpu.with_memory_space_constraint(v, pltpu.HBM) for v in (
        rhs, stiff, jnp.transpose(coupling, (1, 2, 0)), x_in, r_in, p_in, backup_in
    )], beta, fc, bb)
    return pl.pallas_call(
        finish,
        out_shape=(
            pltpu.HBM(field, f32), pltpu.HBM(field, f32), pltpu.HBM((2,) + field, f32),
        ),
        in_specs=[vmem] * 7,
        out_specs=(hbm, hbm, hbm),
        scratch_shapes=[
            pltpu.VMEM(field, f32), pltpu.VMEM(field, f32), pltpu.VMEM(field, f32), dma((10,)),
        ],
        compiler_params=pltpu.CompilerParams(vmem_limit_bytes=8 * 1024 * 1024),
    )(*parts)


def solution(mesh):
    nd, nb = mesh.shape["dom"], mesh.shape["bud"]
    placed = (
        P(None, "dom", "bud", None),
        P("dom", "bud", None),
        P(),
        P(None, "dom", "bud", None),
        P(None, "dom", "bud", None),
        P(None, "dom", "bud", None),
        P(None, None, "dom", "bud", None),
        P(),
        P("dom"),
        P("dom"),
    )
    return jax.shard_map(
        functools.partial(on_device, nd, nb),
        mesh=mesh,
        in_specs=placed,
        out_specs=(
            P(None, "dom", "bud", None),
            P(None, "dom", "bud", None),
            P(None, None, "dom", "bud", None),
        ),
        check_vma=False,
    )
```
